32 devices in a mesh: dp: 4 (over x, core), tensor: 8 (over z, y).
Axes of the slice: x: 2, y: 2, z: 4, core: 2. Of those that a mesh axis runs over, the one named last changes fastest.
Arguments:
- tokens: bfloat16 [12288, 1024], P(('dp', 'tensor')), may hold values from -6 to 6
- seq_ids: int32 [12288], P('dp'), may hold values from 0 to 11, as said below
- blk_ids: int32 [12288], P('dp'), may hold values from 0 to 11, as said below
- norm1_gain: bfloat16 [1024], P('dp'), may hold values from 0.099609375 to 1.8984375
- w_query: bfloat16 [1024, 1024], P('dp', 'tensor'), may hold values from -0.375 to 0.375
- w_key: bfloat16 [1024, 1024], P('dp', 'tensor'), may hold values from -0.1875 to 0.1875
- w_value: bfloat16 [1024, 1024], P('dp', 'tensor'), may hold values from -0.1875 to 0.1875
- w_out: bfloat16 [1024, 1024], P('tensor', 'dp'), may hold values from -0.75 to 0.75
- norm2_gain: bfloat16 [1024], P('dp'), may hold values from 0.099609375 to 1.8984375
- w_gate: bfloat16 [1024, 4096], P('dp', 'tensor'), may hold values from -0.1875 to 0.1875
- w_up: bfloat16 [1024, 4096], P('dp', 'tensor'), may hold values from -0.1875 to 0.1875
- w_down: bfloat16 [4096, 1024], P('tensor', 'dp'), may hold values from -0.09375 to 0.09375
- cotangent: bfloat16 [12288, 1024], P(('dp', 'tensor')), may hold values from -6 to 6
Outputs:
- output: bfloat16 [12288, 1024], P(('dp', 'tensor'))
- input_grad: bfloat16 [12288, 1024], P(('dp', 'tensor'))
- grad_query: float32 [1024, 1024], P('dp', 'tensor')
- grad_key: float32 [1024, 1024], P('dp', 'tensor')
- grad_value: float32 [1024, 1024], P('dp', 'tensor')
- grad_out: float32 [1024, 1024], P('tensor', 'dp')
- grad_gate: float32 [1024, 4096], P('dp', 'tensor')
- grad_up: float32 [1024, 4096], P('dp', 'tensor')
- grad_down: float32 [4096, 1024], P('tensor', 'dp')
- grad_norm1: float32 [1024], P(('dp', 'tensor'))
- grad_norm2: float32 [1024], P(('dp', 'tensor'))
The draws below stay inside these ranges and needn't reach their ends.
Inputs may be any that keep to these rules, and one draw needn't show every extreme that they name: `seq_ids`: sequence ids never fall along the tokens; each sequence is a whole number of aligned runs of 1024 tokens and lies within one aligned run of 3072 tokens. `blk_ids`: the block index of a token is its position within its sequence divided by 256, rounded down.
All inputs are finite; a program needn't handle non-finite values.
Results may differ from the reference program's by a relative error of at most 0.02.
Values may be sent and summed in bfloat16 or wider, within the bound.
No kernel may reach another device: no remote copies, remote signals or barrier semaphores. Data moves between devices by JAX's collectives and lax.ppermute only.
A program may use at most 128 MiB of HBM per device.

```python
import jax
import jax.numpy as jnp
from jax import lax

D = 1024
HEADS = 16
DH = 64
FF = 4096
BLK = 256
MIN_SEQ = 1024
TOK_GRP = 3072
TOKENS = 12288
N_DP = 4


def sequence_layout(key):
    units = TOK_GRP // MIN_SEQ
    groups = TOKENS // TOK_GRP
    coins = jax.random.randint(jax.random.fold_in(key, 11), (groups, units), 0, 2).astype(jnp.int32)
    group_index = jnp.arange(groups, dtype=jnp.int32)[:, None]
    coins = jnp.where(group_index == 0, 0, jnp.where(group_index == groups - 1, 1, coins)).astype(jnp.int32)
    unit_index = jnp.arange(units, dtype=jnp.int32)[None, :]
    begins = jnp.where(unit_index == 0, 1, coins).astype(jnp.int32)
    local_seq = jnp.cumsum(begins, axis=1).astype(jnp.int32) - 1
    unit_seq = local_seq + group_index * units
    first_unit = lax.cummax(jnp.where(begins == 1, unit_index, 0).astype(jnp.int32), axis=1)
    seq_tokens = jnp.repeat(unit_seq, MIN_SEQ, axis=1).reshape(TOKENS)
    first_tokens = jnp.repeat(first_unit, MIN_SEQ, axis=1).reshape(TOKENS)
    position = jnp.arange(TOKENS, dtype=jnp.int32) % TOK_GRP
    block_index = position // BLK - first_tokens * (MIN_SEQ // BLK)
    return (seq_tokens.astype(jnp.int32), block_index.astype(jnp.int32))


def draw_seq_ids(key, part):
    return sequence_layout(key)[0]


def draw_blk_ids(key, part):
    return sequence_layout(key)[1]


def block_scale(key, dims, pieces, low, top_value):
    loudness, own = 1.0, jax.random.fold_in(key, 6)
    for axis_at, parts in pieces:
        draws = jnp.exp(jax.random.uniform(jax.random.fold_in(own, axis_at), (parts,), jnp.float32, low / len(pieces), top_value / len(pieces)))
        loudness = loudness * jnp.repeat(draws, dims[axis_at] // parts).reshape([-1 if axis == axis_at else 1 for axis in range(len(dims))])
    return loudness


def scatter_about(own_key, dims, scale, bound, cuts=(), kind=jnp.bfloat16):
    factor_of = block_scale(own_key, dims, cuts, -0.22, 0.18) if cuts else 1.0
    values = jax.random.normal(own_key, dims, jnp.float32) * scale * factor_of
    return jnp.minimum(jnp.maximum(values, -bound), bound).astype(kind)


def setup_inputs(seed: int = 0) -> dict:
    key_of = jax.random.split(jax.random.key(seed), 14)
    return {
        "tokens": scatter_about(key_of[0], (TOKENS, D), 1.0, 6.0, ((0, 32),)),
        "seq_ids": draw_seq_ids(jax.random.fold_in(key_of[13], 71), 0),
        "blk_ids": draw_blk_ids(jax.random.fold_in(key_of[13], 71), 0),
        "norm1_gain": jnp.clip(1.0 + 0.18 * jax.random.normal(key_of[3], (D,), jnp.float32), 0.099609375, 1.8984375).astype(jnp.bfloat16),
        "w_query": scatter_about(key_of[4], (D, HEADS * DH), (D // 4) ** -0.5, 0.375, ((0, 4), (1, 8))),
        "w_key": scatter_about(key_of[5], (D, HEADS * DH), D ** -0.5, 0.1875, ((0, 4), (1, 8))),
        "w_value": scatter_about(key_of[6], (D, HEADS * DH), D ** -0.5, 0.1875, ((0, 4), (1, 8))),
        "w_out": scatter_about(key_of[7], (HEADS * DH, D), (HEADS * DH // 16) ** -0.5, 0.75, ((0, 8), (1, 4))),
        "norm2_gain": jnp.clip(1.0 + 0.18 * jax.random.normal(key_of[8], (D,), jnp.float32), 0.099609375, 1.8984375).astype(jnp.bfloat16),
        "w_gate": scatter_about(key_of[9], (D, FF), D ** -0.5, 0.1875, ((0, 4), (1, 8))),
        "w_up": scatter_about(key_of[10], (D, FF), D ** -0.5, 0.1875, ((0, 4), (1, 8))),
        "w_down": scatter_about(key_of[11], (FF, D), FF ** -0.5, 0.09375, ((0, 8), (1, 4))),
        "cotangent": scatter_about(key_of[12], (TOKENS, D), 1.0, 6.0, ((0, 32),)),
    }


@jax.custom_vjp
def low(v):
    return lax.optimization_barrier(v.astype(jnp.bfloat16)).astype(jnp.float32)

@jax.custom_vjp
def low_back(v):
    return v

def low_keep(v):
    return (low(v), None)

def low_pass(kept, grad):
    return (grad,)

def back_keep(v):
    return (v, None)

def back_low(kept, grad):
    return (low(grad),)
low.defvjp(low_keep, low_pass)
low_back.defvjp(back_keep, back_low)
EPS = 1e-06
HIGH = lax.Precision.HIGHEST
NEG = -1e+30

def norm_rows(values, gain):
    scale = lax.rsqrt(lax.optimization_barrier(jnp.mean(values * values, axis=-1, keepdims=True)) + EPS)
    return values * scale * gain

def attend(normed, w_query, w_key, w_value, w_out, seq_ids, blk_ids):
    rows = normed.shape[0]
    queries = low_back(low(jnp.dot(normed, w_query, precision=HIGH))).reshape(rows, HEADS, DH)
    keys = low_back(low(jnp.dot(normed, w_key, precision=HIGH))).reshape(rows, HEADS, DH)
    values = low_back(low(jnp.dot(normed, w_value, precision=HIGH))).reshape(rows, HEADS, DH)
    block = min(512, rows)

    def one_block(start):
        query_block = lax.dynamic_slice_in_dim(queries, start, block, 0)
        query_seq = lax.dynamic_slice_in_dim(seq_ids, start, block, 0)
        query_blk = lax.dynamic_slice_in_dim(blk_ids, start, block, 0)
        allowed = (query_seq[:, None] == seq_ids[None, :]) & (blk_ids[None, :] <= query_blk[:, None])
        scores = jnp.einsum('qhd,khd->hqk', query_block, keys, precision=HIGH) * DH ** (-0.5)
        scores = low_back(scores)
        scores = jnp.where(allowed[None], scores, NEG)
        probs = jax.nn.softmax(scores, axis=-1)
        mixed = jnp.einsum('hqk,khd->qhd', low(probs), values, precision=HIGH)
        return mixed.reshape(block, HEADS * DH)
    starts = jnp.arange(rows // block, dtype=jnp.int32) * block
    attended = lax.map(jax.checkpoint(one_block), starts).reshape(rows, HEADS * DH)
    attended = low_back(low(attended))
    return jnp.dot(attended, w_out, precision=HIGH)

def layer(tokens, norm1_gain, w_query, w_key, w_value, w_out, norm2_gain, w_gate, w_up, w_down, seq_ids, blk_ids):

    def one_group(group):
        resid, group_seq, group_blk = group
        normed_first = low(norm_rows(resid, norm1_gain))
        mixed = resid + low_back(attend(normed_first, w_query, w_key, w_value, w_out, group_seq, group_blk))
        normed_second = low(norm_rows(mixed, norm2_gain))
        gate = low_back(jnp.dot(normed_second, w_gate, precision=HIGH))
        upward = low_back(jnp.dot(normed_second, w_up, precision=HIGH))
        hidden = low(jax.nn.silu(gate) * upward)
        return mixed + jnp.dot(hidden, w_down, precision=HIGH)
    grouped = (tokens.reshape(N_DP, TOK_GRP, D), seq_ids.reshape(N_DP, TOK_GRP), blk_ids.reshape(N_DP, TOK_GRP))
    return lax.map(jax.checkpoint(one_group), grouped).reshape(TOKENS, D)

def reference(tokens, seq_ids, blk_ids, norm1_gain, w_query, w_key, w_value, w_out, norm2_gain, w_gate, w_up, w_down, cotangent):
    floats = tuple((item.astype(jnp.float32) for item in (tokens, norm1_gain, w_query, w_key, w_value, w_out, norm2_gain, w_gate, w_up, w_down)))

    def forward(*params):
        return layer(*params, seq_ids, blk_ids)
    result, pullback = jax.vjp(forward, *floats)
    grads = pullback(cotangent.astype(jnp.float32))
    grad_tokens, grad_norm1, grad_query, grad_key, grad_value, grad_out, grad_norm2, grad_gate, grad_up, grad_down = grads
    return (result.astype(jnp.bfloat16), grad_tokens.astype(jnp.bfloat16), grad_query, grad_key, grad_value, grad_out, grad_gate, grad_up, grad_down, grad_norm1, grad_norm2)
```

```python
import functools

import jax
import jax.numpy as jnp
from jax import lax
from jax.experimental import pallas as pl
from jax.experimental.pallas import tpu as pltpu
from jax.sharding import PartitionSpec as P

DH = 64
BLK = 256
EPS = 1e-06
HT = 256
NT = (((1,), (1,)), ((), ()))
NN = (((1,), (0,)), ((), ()))
TN = (((0,), (0,)), ((), ()))


def dot(a, b, dims):
    return lax.dot_general(a, b, dims, preferred_element_type=jnp.float32)


def split_heads(block):
    low = lax.broadcasted_iota(jnp.int32, block.shape, 1) < DH
    zero = jnp.zeros_like(block)
    return jnp.concatenate([jnp.where(low, block, zero), jnp.where(low, zero, block)], axis=0)


def scaled_q(qkv_ref, rows):
    return split_heads((qkv_ref[rows, 0:128].astype(jnp.float32) * DH ** -0.5).astype(jnp.bfloat16))


def attn_fwd_kernel(first_ref, qkv_ref, out_ref, log_ref, vt_ref, top_ref, sum_ref, acc_ref):
    i = pl.program_id(0)
    @pl.when(i == 0)
    def _():
        vt_ref[...] = jnp.transpose(qkv_ref[:, 256:384])
    rows = pl.ds(pl.multiple_of(i * BLK, BLK), BLK)
    both = scaled_q(qkv_ref, rows)
    top_ref[...] = jnp.full_like(top_ref, -1e30)
    sum_ref[...] = jnp.zeros_like(sum_ref)
    acc_ref[...] = jnp.zeros_like(acc_ref)

    def step(j, _):
        at = pl.ds(pl.multiple_of(j * BLK, BLK), BLK)
        scores = dot(qkv_ref[at, 128:256], both, NT)
        old = top_ref[...]
        new = jnp.maximum(old, jnp.max(scores, axis=0, keepdims=True))
        top_ref[...] = new
        weights = jnp.exp(scores - new)
        shrink = jnp.exp(old - new)
        sum_ref[...] = sum_ref[...] * shrink + jnp.sum(weights, axis=0, keepdims=True)
        probs = weights.astype(jnp.bfloat16)
        acc_ref[:, 0:BLK] = acc_ref[:, 0:BLK] * shrink[:, 0:BLK] + dot(vt_ref[0:DH, at], probs[:, 0:BLK], NN)
        acc_ref[:, BLK:] = acc_ref[:, BLK:] * shrink[:, BLK:] + dot(vt_ref[DH:, at], probs[:, BLK:], NN)
        return 0

    lax.fori_loop(first_ref[i], i + 1, step, 0)
    mixed = acc_ref[...] / sum_ref[...]
    out_ref[...] = jnp.transpose(jnp.concatenate([mixed[:, 0:BLK], mixed[:, BLK:]], axis=0)).astype(jnp.bfloat16)
    log_ref[0] = top_ref[...] + jnp.log(sum_ref[...])


def attn_fwd(qkv, first):
    rows = qkv.shape[0]
    n = rows // BLK
    return pl.pallas_call(
        attn_fwd_kernel, name="attn_fwd",
        out_shape=(jax.ShapeDtypeStruct((rows,128),jnp.bfloat16), jax.ShapeDtypeStruct((n,1,2*BLK),jnp.float32)),
        grid_spec=pltpu.PrefetchScalarGridSpec(
            num_scalar_prefetch=1, grid=(n,),
            in_specs=[pl.BlockSpec((rows,384), lambda i,s:(0,0))],
            out_specs=[pl.BlockSpec((BLK,128), lambda i,s:(i,0)), pl.BlockSpec((1,1,2*BLK), lambda i,s:(i,0,0))],
            scratch_shapes=[pltpu.VMEM((128,rows),jnp.bfloat16), pltpu.VMEM((1,2*BLK),jnp.float32), pltpu.VMEM((1,2*BLK),jnp.float32), pltpu.VMEM((DH,2*BLK),jnp.float32)]),
        compiler_params=pltpu.CompilerParams(vmem_limit_bytes=32<<20),
        cost_estimate=pl.CostEstimate(flops=10*10**9, bytes_accessed=5*10**6, transcendentals=10**7),
    )(first, qkv)


def attn_bwd_kernel(first_ref, qkv_ref, do_ref, o_ref, log_ref, out_ref, kt_ref, dk_ref, dv_ref, dq_ref):
    i = pl.program_id(0)
    @pl.when(i == 0)
    def _():
        kt_ref[...] = jnp.transpose(qkv_ref[:, 128:256])
        dk_ref[...] = jnp.zeros_like(dk_ref)
        dv_ref[...] = jnp.zeros_like(dv_ref)
    rows = pl.ds(pl.multiple_of(i * BLK, BLK), BLK)
    both = scaled_q(qkv_ref, rows)
    grads = split_heads(do_ref[...])
    outs = o_ref[...].astype(jnp.float32)
    product = grads.astype(jnp.float32) * jnp.concatenate([outs, outs], axis=0)
    delta = lax.dot_general(jnp.ones((8, 128), jnp.float32), product, NT, precision=lax.Precision.HIGHEST, preferred_element_type=jnp.float32)[0:1]
    logs = log_ref[0]
    dq_ref[...] = jnp.zeros_like(dq_ref)

    def step(j, _):
        at = pl.ds(pl.multiple_of(j * BLK, BLK), BLK)
        probs = jnp.exp(dot(qkv_ref[at, 128:256], both, NT) - logs)
        dp = dot(qkv_ref[at, 256:384], grads, NT)
        ds = (probs * (dp - delta)).astype(jnp.bfloat16)
        dv_ref[at, :] += dot(probs.astype(jnp.bfloat16), grads, NN)
        dk_ref[at, :] += dot(ds, both, NN)
        dq_ref[:, 0:BLK] += dot(kt_ref[0:DH, at], ds[:, 0:BLK], NN)
        dq_ref[:, BLK:] += dot(kt_ref[DH:, at], ds[:, BLK:], NN)
        return 0

    lax.fori_loop(first_ref[i], i + 1, step, 0)
    dq = jnp.concatenate([dq_ref[:, 0:BLK], dq_ref[:, BLK:]], axis=0)
    out_ref[rows, 0:128] = (jnp.transpose(dq) * DH ** -0.5).astype(jnp.bfloat16)

    @pl.when(i == pl.num_programs(0) - 1)
    def _():
        out_ref[:, 128:256] = dk_ref[...].astype(jnp.bfloat16)
        out_ref[:, 256:384] = dv_ref[...].astype(jnp.bfloat16)


def attn_bwd(qkv, do, o, log, first):
    rows = qkv.shape[0]
    n = rows // BLK
    blk = pl.BlockSpec((BLK,128), lambda i,s:(i,0))
    return pl.pallas_call(
        attn_bwd_kernel, name="attn_bwd",
        out_shape=jax.ShapeDtypeStruct((rows,384),jnp.bfloat16),
        grid_spec=pltpu.PrefetchScalarGridSpec(
            num_scalar_prefetch=1, grid=(n,),
            in_specs=[pl.BlockSpec((rows,384), lambda i,s:(0,0)), blk, blk, pl.BlockSpec((1,1,2*BLK), lambda i,s:(i,0,0))],
            out_specs=pl.BlockSpec((rows,384), lambda i,s:(0,0)),
            scratch_shapes=[pltpu.VMEM((128,rows),jnp.bfloat16), pltpu.VMEM((rows,128),jnp.float32), pltpu.VMEM((rows,128),jnp.float32), pltpu.VMEM((DH,2*BLK),jnp.float32)]),
        compiler_params=pltpu.CompilerParams(vmem_limit_bytes=40<<20),
        cost_estimate=pl.CostEstimate(flops=26*10**9, bytes_accessed=9*10**6, transcendentals=10**7),
    )(first, qkv, do, o, log)


def ffn_kernel(n_ref, c_ref, w_ref, f_ref, d_ref, z_ref, g_ref, u_ref):
    n2, c = n_ref[0], c_ref[0]
    wg, wu, wd = w_ref[0], w_ref[1], w_ref[2]
    gate, up, dz = dot(n2, wg, NT), dot(n2, wu, NT), dot(c, wd, NT)
    sig = jax.nn.sigmoid(gate)
    silu = gate * sig
    z = (silu * up).astype(jnp.bfloat16)
    dg = (dz * up * (sig * (1.0 + gate * (1.0 - sig)))).astype(jnp.bfloat16)
    du = (dz * silu).astype(jnp.bfloat16)
    z_ref[0] = z
    g_ref[0] = dg
    u_ref[0] = du
    f_ref[0] = dot(z, wd, NN).astype(jnp.bfloat16)
    d_ref[0] = (dot(dg, wg, NN) + dot(du, wu, NN)).astype(jnp.bfloat16)


def ffn(n2, c, w):
    nb, rows, width = n2.shape; hid = w.shape[1]
    full = pl.BlockSpec((1,rows,width), lambda s:(s,0,0))
    col = pl.BlockSpec((1,rows,hid), lambda s:(s,0,0))
    bf = jnp.bfloat16
    return pl.pallas_call(
        ffn_kernel, name="ffn",
        grid=(nb,),
        out_shape=[jax.ShapeDtypeStruct((nb,rows,width),bf)]*2+[jax.ShapeDtypeStruct((nb,rows,hid),bf)]*3,
        in_specs=[full]*2+[pl.BlockSpec((3,hid,width), lambda s:(0,0,0), pipeline_mode=pl.Buffered(1))],
        out_specs=[full]*2+[col]*3,
        compiler_params=pltpu.CompilerParams(vmem_limit_bytes=56<<20),
        cost_estimate=pl.CostEstimate(flops=2*nb*rows*width*hid*6, bytes_accessed=20*10**6, transcendentals=nb*rows*hid),
    )(n2,c,w)


def ffn_grad_kernel(nb, *refs):
    ns, cs, zs, gs, us = (refs[k*nb:(k+1)*nb] for k in range(5))
    out = refs[5*nb]
    for which, (left, right) in enumerate(((gs, ns), (us, ns), (zs, cs))):
        total = dot(left[0][...], right[0][...], TN)
        for b in range(1, nb):
            total += dot(left[b][...], right[b][...], TN)
        out[which] = total.astype(jnp.bfloat16)


def ffn_grad(ns, cs, zs, gs, us):
    nb = len(ns); rows, width = ns[0].shape; hid = zs[0].shape[1]
    full = pl.BlockSpec((rows,width), lambda s:(0,0))
    col = pl.BlockSpec((rows,HT), lambda s:(0,s))
    return pl.pallas_call(
        functools.partial(ffn_grad_kernel, nb), name="ffn_grad",
        grid=(hid//HT,),
        out_shape=jax.ShapeDtypeStruct((3,hid,width),jnp.bfloat16),
        in_specs=[full]*(2*nb)+[col]*(3*nb),
        out_specs=pl.BlockSpec((3,HT,width), lambda s:(0,s,0)),
        compiler_params=pltpu.CompilerParams(vmem_limit_bytes=56<<20),
        cost_estimate=pl.CostEstimate(flops=2*nb*rows*width*hid*3, bytes_accessed=20*10**6, transcendentals=0),
    )(*ns,*cs,*zs,*gs,*us)


def row_scale(values):
    return lax.rsqrt(jnp.mean(values * values, axis=-1, keepdims=True) + EPS)


def norm_back(grad_normed, values, scale, gain):
    weighted = grad_normed * gain
    inner = jnp.mean(weighted * values, axis=-1, keepdims=True)
    return scale * weighted - values * (scale * scale * scale) * inner


def make(n_dp, n_t):
    ring = list(range(0, n_t, 2)) + list(range(n_t - 1, 0, -2))
    bf = jnp.bfloat16

    def hop(value, k):
        return lax.ppermute(value, "tensor", [(ring[i], ring[(i + k) % n_t]) for i in range(n_t)])

    def flip(value, k):
        return lax.ppermute(value, "dp", [(i, i ^ k) for i in range(n_dp)])

    bits = [1 << b for b in range(n_dp.bit_length() - 1)]
    n_ff = min(n_dp, 4)
    ff_bits = [b for b in bits if b < n_ff]

    def put(buf, piece, start, axis):
        return lax.dynamic_update_slice_in_dim(buf, piece, start, axis)

    def take(buf, start, size, axis):
        return lax.dynamic_slice_in_dim(buf, start, size, axis)

    def gather_dp(piece, axis, me):
        size = piece.shape[axis]
        shape = list(piece.shape)
        shape[axis] = size * n_dp
        buf = put(jnp.zeros(shape, piece.dtype), piece, me * size, axis)
        for k in range(1, n_dp):
            buf = put(buf, flip(piece, k), (me ^ k) * size, axis)
        return buf

    def scatter_sum_dp(whole, axis, me):
        size = whole.shape[axis] // n_dp
        shape = whole.shape
        core = whole.reshape(shape[:axis] + (n_dp, size) + shape[axis + 1 :])
        left = n_dp
        for bit in bits:
            now = core.reshape(core.shape[:axis] + (left // 2, 2) + core.shape[axis + 1 :])
            side = (me // bit) % 2
            keep = lax.dynamic_index_in_dim(now, side, axis + 1, keepdims=False)
            send = lax.dynamic_index_in_dim(now, 1 - side, axis + 1, keepdims=False)
            core = keep + flip(send.astype(bf), bit).astype(jnp.float32)
            left //= 2
        return core.reshape(shape[:axis] + (size,) + shape[axis + 1 :])

    def scatter_sum_all(total, d, at):
        width = total.shape[0] // (n_dp * n_t)
        parts = total.reshape(n_dp, n_t, width)
        own = lax.dynamic_index_in_dim(parts, d, 0, keepdims=False)
        for k in range(1, n_dp):
            own = own + flip(lax.dynamic_index_in_dim(parts, d ^ k, 0, keepdims=False), k)
        mine = lax.dynamic_index_in_dim(own, at[0], 0, keepdims=False)
        for j in range(1, n_t):
            mine = mine + hop(lax.dynamic_index_in_dim(own, at[j], 0, keepdims=False), j)
        return mine

    def on_device(
        tokens, seq_ids, blk_ids, norm1_gain, w_query, w_key, w_value, w_out, norm2_gain,
        w_gate, w_up, w_down, cotangent,
    ):
        d = lax.axis_index("dp")
        t = lax.axis_index("tensor")
        half_t = n_t // 2
        pos = jnp.where(t % 2 == 0, t // 2, n_t - 1 - t // 2)

        def owner(p):
            p = lax.rem(p + 2 * n_t, n_t)
            return jnp.where(p < half_t, 2 * p, 2 * (n_t - 1 - p) + 1)

        ahead = [owner(pos + j) for j in range(n_t)]
        behind = [owner(pos - j) for j in range(n_t)]
        own_rows, width = tokens.shape
        rows = own_rows * n_t
        half = own_rows // 2
        part = width // n_dp

        gains = gather_dp(jnp.stack([norm1_gain, norm2_gain]), 1, d).astype(jnp.float32)
        gain1, gain2 = gains[0:1], gains[1:2]
        w_qkv = gather_dp(jnp.concatenate([w_query, w_key, w_value], axis=1), 0, d)
        resid = tokens.astype(jnp.float32)
        scale1 = row_scale(resid)
        normed1 = (resid * scale1 * gain1).astype(bf)

        all1 = put(jnp.zeros((rows, width), bf), normed1, t * own_rows, 0)
        up_going, down_going = normed1[:half], normed1[half:]
        for k in range(1, n_t):
            up_going = hop(up_going, 1)
            down_going = hop(down_going, -1)
            all1 = put(all1, up_going, behind[k] * own_rows, 0)
            all1 = put(all1, down_going, ahead[k] * own_rows + half, 0)
        qkv = jnp.dot(all1, w_qkv, preferred_element_type=jnp.float32).astype(bf)

        def gather_slots(value):
            acc, ids = value[None], [0]
            for bit in ff_bits[:0:-1]:
                acc = jnp.concatenate([acc, flip(acc, bit)])
                ids = ids + [k ^ bit for k in ids]
            return acc, ids

        hid_t = w_down.shape[0]
        hid = hid_t // n_ff
        shards = jnp.stack([w_gate.T, w_up.T, w_down]).reshape(3, n_ff, hid, part)
        own_w = jnp.zeros((3, hid, width), bf)
        for k in range(n_dp):
            piece = lax.dynamic_index_in_dim(shards, (d ^ k) % n_ff, 1, keepdims=False)
            own_w = put(own_w, flip(piece, k) if k else piece, (d ^ k) * part, 2)
        out_rows = gather_dp(w_out, 1, d)
        out_half = w_out.shape[0] // 2
        core = d % 2
        own_o = take(out_rows, core * out_half, out_half, 0)
        own_w, own_o, all1 = lax.optimization_barrier((own_w, own_o, all1))

        def ring_slots(block, axis):
            cut = block.shape[axis] // 2
            one = lax.slice_in_dim(block, 0, cut, axis=axis)
            two = lax.slice_in_dim(block, cut, 2 * cut, axis=axis)
            out = [(one, two)]
            for _ in range(1, n_t):
                one, two = hop(one, 1), hop(two, -1)
                out.append((one, two))
            return out

        o_slots = ring_slots(own_o, 0)
        o_mine = jnp.concatenate(
            [piece for j in range(n_t) for piece in (o_slots[(n_t - j) % n_t][0], o_slots[j][1])]
        ).reshape(n_t, out_half, width)
        o_peer = flip(o_mine, 1)
        out_full = jnp.where(
            core == 0,
            jnp.concatenate([o_mine, o_peer], axis=1),
            jnp.concatenate([o_peer, o_mine], axis=1),
        ).reshape(n_t * 2 * out_half, width)
        w_slots = ring_slots(own_w, 1)
        weights = jnp.concatenate([piece for pair in w_slots for piece in pair], axis=1)

        units = seq_ids.reshape(-1, 4 * BLK)[:, 0]
        n_units = rows // (4 * BLK)
        same = units[:, None] == units[None, :]
        first_unit = jnp.min(jnp.where(same, jnp.arange(n_units)[None, :], n_units), axis=1)
        first = jnp.repeat(first_unit * 4, 4).astype(jnp.int32)
        attended, logs = attn_fwd(qkv, first)

        mixed_cols = [take(attended, t * own_rows, own_rows, 0)]
        for j in range(1, n_t):
            mixed_cols.append(hop(take(attended, behind[j] * own_rows, own_rows, 0), -j))
        heads_own = jnp.concatenate(mixed_cols, axis=1)
        mixed = resid + jnp.dot(heads_own, out_full, preferred_element_type=jnp.float32)
        scale2 = row_scale(mixed)
        normed2 = (mixed * scale2 * gain2).astype(bf)

        c_slots, ids = gather_slots(cotangent)
        n_slots, _ = gather_slots(normed2)
        c_near = jnp.concatenate([c_slots[:1], flip(c_slots[:1], 1)])
        n_near = jnp.concatenate([n_slots[:1], flip(n_slots[:1], 1)])
        c_far = jnp.concatenate([c_slots[1:], flip(c_slots[1:], 1)])
        n_far = jnp.concatenate([n_slots[1:], flip(n_slots[1:], 1)])
        f_near, d_near, z_near, g_near, u_near = ffn(n_near, c_near, weights)
        f_far, d_far, z_far, g_far, u_far = ffn(n_far, c_far, weights)

        def back_slots(near, far):
            f32 = jnp.float32
            n_far_slots = far.shape[0] // 2
            far_sum = far[:n_far_slots].astype(f32) + flip(far[n_far_slots:], 1).astype(f32)
            near_sum = near[:1].astype(f32) + flip(near[1:], 1).astype(f32)
            acc = jnp.concatenate([near_sum, far_sum])
            for bit in ff_bits[1:]:
                cut = acc.shape[0] // 2
                acc = acc[:cut] + flip(acc[cut:].astype(bf), bit).astype(f32)
            return acc[0]

        grad_normed2 = back_slots(d_near, d_far)
        ffn_total = back_slots(f_near, f_far)
        output = (mixed + ffn_total).astype(bf)
        grad_w = ffn_grad(
            [n_near.reshape(-1, width), n_far.reshape(-1, width)],
            [c_near.reshape(-1, width), c_far.reshape(-1, width)],
            [z.reshape(-1, z.shape[-1]) for z in (z_near, z_far)],
            [g.reshape(-1, g.shape[-1]) for g in (g_near, g_far)],
            [u.reshape(-1, u.shape[-1]) for u in (u_near, u_far)],
        )

        cot = cotangent.astype(jnp.float32)
        grad_mixed = cot + norm_back(grad_normed2, mixed, scale2, gain2)
        grad_gain2 = jnp.sum(grad_normed2 * mixed * scale2, axis=0)
        grad_bf = grad_mixed.astype(bf)
        grad_heads = lax.dot_general(
            grad_bf, out_full, NT, preferred_element_type=jnp.float32
        ).astype(bf)
        wide = 2 * out_half
        grad_att = put(
            jnp.zeros((rows, wide), bf), grad_heads[:, :wide], t * own_rows, 0
        )
        for j in range(1, n_t):
            piece = hop(grad_heads[:, j * wide : (j + 1) * wide], j)
            grad_att = put(grad_att, piece, behind[j] * own_rows, 0)
        grad_qkv = attn_bwd(qkv, grad_att, attended, logs, first)

        back_rows = lax.dot_general(
            grad_qkv, w_qkv, NT, preferred_element_type=jnp.float32
        ).astype(bf)

        def rows_of(which, low):
            return take(back_rows, which * own_rows + (0 if low else half), half, 0)

        one, two = rows_of(behind[n_t - 1], True), rows_of(ahead[n_t - 1], False)
        for k in range(n_t - 2, -1, -1):
            one = hop(one, -1).astype(jnp.float32) + rows_of(behind[k], True).astype(jnp.float32)
            two = hop(two, 1).astype(jnp.float32) + rows_of(ahead[k], False).astype(jnp.float32)
            if k:
                one, two = one.astype(bf), two.astype(bf)
        grad_normed1 = jnp.concatenate([one, two])
        input_grad = (grad_mixed + norm_back(grad_normed1, resid, scale1, gain1)).astype(bf)
        grad_gain1 = jnp.sum(grad_normed1 * resid * scale1, axis=0)

        grad_wqkv = lax.dot_general(all1, grad_qkv, TN, preferred_element_type=jnp.float32)
        grad_wqkv = scatter_sum_dp(grad_wqkv, 0, d)
        grad_query, grad_key, grad_value = jnp.split(grad_wqkv, 3, axis=1)

        grad_wo = lax.dot_general(heads_own, grad_bf, TN, preferred_element_type=jnp.float32)
        grad_wo = scatter_sum_dp(grad_wo, 1, d).astype(bf).reshape(n_t, wide, part)
        grad_out = grad_wo[0].astype(jnp.float32)
        for j in range(1, n_t):
            grad_out = grad_out + hop(grad_wo[j], j).astype(jnp.float32)

        cut = hid // 2
        g_slots = grad_w.reshape(3, n_t, 2, cut, width)
        one, two = g_slots[:, n_t - 1, 0], g_slots[:, n_t - 1, 1]
        for k in range(n_t - 2, -1, -1):
            one = (hop(one, -1).astype(jnp.float32) + g_slots[:, k, 0].astype(jnp.float32)).astype(bf)
            two = (hop(two, 1).astype(jnp.float32) + g_slots[:, k, 1].astype(jnp.float32)).astype(bf)
        summed = jnp.concatenate([one, two], axis=1).reshape(3, hid, n_dp, part)
        full = jnp.zeros((3, n_ff, hid, part), jnp.float32)
        for k in range(n_ff):
            total = 0.0
            for far in range(k, n_dp, n_ff):
                piece = lax.dynamic_index_in_dim(summed, d ^ far, 2, keepdims=False)[:, None]
                total = total + (flip(piece, far) if far else piece).astype(jnp.float32)
            full = put(full, total, (d ^ k) % n_ff, 1)
        full = full.reshape(3, hid_t, part)
        grad_gate, grad_up, grad_down = full[0].T, full[1].T, full[2]

        grad_norm1 = scatter_sum_all(grad_gain1, d, [t] + ahead[1:])
        grad_norm2 = scatter_sum_all(grad_gain2, d, [t] + ahead[1:])
        return (
            output, input_grad, grad_query, grad_key, grad_value, grad_out,
            grad_gate, grad_up, grad_down, grad_norm1, grad_norm2,
        )

    return on_device


def solution(mesh):
    rows = P(("dp", "tensor"), None)
    return jax.shard_map(
        make(mesh.shape["dp"], mesh.shape["tensor"]),
        mesh=mesh,
        in_specs=(
            rows, P("dp"), P("dp"), P("dp"), P("dp", "tensor"), P("dp", "tensor"),
            P("dp", "tensor"), P("tensor", "dp"), P("dp"), P("dp", "tensor"),
            P("dp", "tensor"), P("tensor", "dp"), rows,
        ),
        out_specs=(
            rows, rows, P("dp", "tensor"), P("dp", "tensor"), P("dp", "tensor"),
            P("tensor", "dp"), P("dp", "tensor"), P("dp", "tensor"), P("tensor", "dp"),
            P(("dp", "tensor")), P(("dp", "tensor")),
        ),
        check_vma=False,
    )
```

```python
import functools

import jax
import jax.numpy as jnp
from jax import lax
from jax.experimental import pallas as pl
from jax.experimental.pallas import tpu as pltpu
from jax.sharding import PartitionSpec as P

DH = 64
BLK = 256
EPS = 1e-06
HT = 256
BULK_AT = 5
WEIGHTS_AT = 3
RS_LATE = True
NT = (((1,), (1,)), ((), ()))
NN = (((1,), (0,)), ((), ()))
TN = (((0,), (0,)), ((), ()))


def dot(a, b, dims):
    return lax.dot_general(a, b, dims, preferred_element_type=jnp.float32)


def split_heads(block):
    low = lax.broadcasted_iota(jnp.int32, block.shape, 1) < DH
    zero = jnp.zeros_like(block)
    return jnp.concatenate([jnp.where(low, block, zero), jnp.where(low, zero, block)], axis=0)


def scaled_q(qkv_ref, rows):
    return split_heads((qkv_ref[rows, 0:128].astype(jnp.float32) * DH ** -0.5).astype(jnp.bfloat16))


def in_pairs(first, last, ahead, work):
    count = last - first + 1
    ahead(first, 0)

    def pair(p, _):
        j = first + 2 * p
        ahead(j + 1, 1)
        work(j, 0)
        ahead(jnp.minimum(j + 2, last), 0)
        work(j + 1, 1)
        return 0

    lax.fori_loop(0, count // 2, pair, 0)

    @pl.when(count % 2 == 1)
    def _():
        work(last, 0)


def attn_fwd_kernel(first_ref, qkv_ref, out_ref, log_ref, vt_ref, top_ref, sum_ref, acc_ref, qt_ref, *score_refs):
    i = pl.program_id(0)
    @pl.when(i == 0)
    def _():
        vt_ref[...] = jnp.transpose(qkv_ref[:, 256:384])
    rows = pl.ds(pl.multiple_of(i * BLK, BLK), BLK)
    qt_ref[...] = jnp.transpose(scaled_q(qkv_ref, rows))
    top_ref[...] = jnp.full_like(top_ref, -1e30)
    sum_ref[...] = jnp.zeros_like(sum_ref)
    acc_ref[...] = jnp.zeros_like(acc_ref)

    def ahead(j, slot):
        at = pl.ds(pl.multiple_of(j * BLK, BLK), BLK)
        score_refs[slot][...] = dot(qkv_ref[at, 128:256], qt_ref[...], NN)

    def work(j, slot):
        at = pl.ds(pl.multiple_of(j * BLK, BLK), BLK)
        scores = score_refs[slot][...]
        old = top_ref[...]
        new = jnp.maximum(old, jnp.max(scores, axis=0, keepdims=True))
        top_ref[...] = new
        weights = jnp.exp(scores - new)
        shrink = jnp.exp(old - new)
        sum_ref[...] = sum_ref[...] * shrink + jnp.sum(weights, axis=0, keepdims=True)
        probs = weights.astype(jnp.bfloat16)
        acc_ref[:, 0:BLK] = acc_ref[:, 0:BLK] * shrink[:, 0:BLK] + dot(vt_ref[0:DH, at], probs[:, 0:BLK], NN)
        acc_ref[:, BLK:] = acc_ref[:, BLK:] * shrink[:, BLK:] + dot(vt_ref[DH:, at], probs[:, BLK:], NN)

    in_pairs(first_ref[i], i, ahead, work)
    mixed = acc_ref[...] / sum_ref[...]
    out_ref[...] = jnp.transpose(jnp.concatenate([mixed[:, 0:BLK], mixed[:, BLK:]], axis=0)).astype(jnp.bfloat16)
    log_ref[0] = top_ref[...] + jnp.log(sum_ref[...])


def attn_fwd(qkv, first):
    rows = qkv.shape[0]
    n = rows // BLK
    f32 = jnp.float32
    return pl.pallas_call(
        attn_fwd_kernel, name="attn_fwd",
        out_shape=(jax.ShapeDtypeStruct((rows,128),jnp.bfloat16), jax.ShapeDtypeStruct((n,1,2*BLK),f32)),
        grid_spec=pltpu.PrefetchScalarGridSpec(
            num_scalar_prefetch=1, grid=(n,),
            in_specs=[pl.BlockSpec((rows,384), lambda i,s:(0,0))],
            out_specs=[pl.BlockSpec((BLK,128), lambda i,s:(i,0)), pl.BlockSpec((1,1,2*BLK), lambda i,s:(i,0,0))],
            scratch_shapes=[pltpu.VMEM((128,rows),jnp.bfloat16), pltpu.VMEM((1,2*BLK),f32), pltpu.VMEM((1,2*BLK),f32), pltpu.VMEM((DH,2*BLK),f32),pltpu.VMEM((128,2*BLK),jnp.bfloat16)]+[pltpu.VMEM((BLK,2*BLK),f32)]*2),
        compiler_params=pltpu.CompilerParams(vmem_limit_bytes=32<<20),
        cost_estimate=pl.CostEstimate(flops=10*10**9, bytes_accessed=5*10**6, transcendentals=10**7),
    )(first, qkv)


def attn_bwd_kernel(first_ref, qkv_ref, do_ref, o_ref, log_ref, out_ref, kt_ref, dk_ref, dv_ref, dq_ref, qt_ref, gt_ref, *score_refs):
    i = pl.program_id(0)
    @pl.when(i == 0)
    def _():
        kt_ref[...] = jnp.transpose(qkv_ref[:, 128:256])
        dk_ref[...] = jnp.zeros_like(dk_ref)
        dv_ref[...] = jnp.zeros_like(dv_ref)
    rows = pl.ds(pl.multiple_of(i * BLK, BLK), BLK)
    both = scaled_q(qkv_ref, rows)
    grads = split_heads(do_ref[...])
    logs = log_ref[0]
    qt_ref[...] = jnp.transpose(both)
    turned = jnp.transpose(grads)
    gt_ref[...] = turned
    outs = jnp.transpose(o_ref[...]).astype(jnp.float32)
    delta = jnp.sum(turned.astype(jnp.float32) * jnp.concatenate([outs, outs], axis=1), axis=0, keepdims=True)
    dq_ref[...] = jnp.zeros_like(dq_ref)

    def ahead(j, slot):
        at = pl.ds(pl.multiple_of(j * BLK, BLK), BLK)
        score_refs[slot][...] = dot(qkv_ref[at, 128:256], qt_ref[...], NN)
        score_refs[2 + slot][...] = dot(qkv_ref[at, 256:384], gt_ref[...], NN)

    def work(j, slot):
        at = pl.ds(pl.multiple_of(j * BLK, BLK), BLK)
        probs = jnp.exp(score_refs[slot][...] - logs)
        ds = (probs * (score_refs[2 + slot][...] - delta)).astype(jnp.bfloat16)
        dv_ref[at, :] += dot(probs.astype(jnp.bfloat16), grads, NN)
        dk_ref[at, :] += dot(ds, both, NN)
        dq_ref[:, 0:BLK] += dot(kt_ref[0:DH, at], ds[:, 0:BLK], NN)
        dq_ref[:, BLK:] += dot(kt_ref[DH:, at], ds[:, BLK:], NN)

    in_pairs(first_ref[i], i, ahead, work)
    dq = jnp.concatenate([dq_ref[:, 0:BLK], dq_ref[:, BLK:]], axis=0)
    out_ref[rows, 0:128] = (jnp.transpose(dq) * DH ** -0.5).astype(jnp.bfloat16)

    @pl.when(i == pl.num_programs(0) - 1)
    def _():
        out_ref[:, 128:256] = dk_ref[...].astype(jnp.bfloat16)
        out_ref[:, 256:384] = dv_ref[...].astype(jnp.bfloat16)


def attn_bwd(qkv, do, o, log, first):
    rows = qkv.shape[0]
    n = rows // BLK
    f32 = jnp.float32
    blk = pl.BlockSpec((BLK,128), lambda i,s:(i,0))
    return pl.pallas_call(
        attn_bwd_kernel, name="attn_bwd",
        out_shape=jax.ShapeDtypeStruct((rows,384),jnp.bfloat16),
        grid_spec=pltpu.PrefetchScalarGridSpec(
            num_scalar_prefetch=1, grid=(n,),
            in_specs=[pl.BlockSpec((rows,384), lambda i,s:(0,0)), blk, blk, pl.BlockSpec((1,1,2*BLK), lambda i,s:(i,0,0))],
            out_specs=pl.BlockSpec((rows,384), lambda i,s:(0,0)),
            scratch_shapes=[pltpu.VMEM((128,rows),jnp.bfloat16), pltpu.VMEM((rows,128),f32), pltpu.VMEM((rows,128),f32), pltpu.VMEM((DH,2*BLK),f32)]+[pltpu.VMEM((128,2*BLK),jnp.bfloat16)]*2+[pltpu.VMEM((BLK,2*BLK),f32)]*4),
        compiler_params=pltpu.CompilerParams(vmem_limit_bytes=40<<20),
        cost_estimate=pl.CostEstimate(flops=26*10**9, bytes_accessed=9*10**6, transcendentals=10**7),
    )(first, qkv, do, o, log)


def ffn_kernel(n_ref, c_ref, gate_ref, up_ref, down_ref, f_ref, d_ref, z_ref, g_ref, u_ref):
    n2, c = n_ref[0], c_ref[0]
    wg, wu, wd = (ref[...].reshape(-1, n2.shape[1]) for ref in (gate_ref, up_ref, down_ref))
    gate, up, dz = dot(n2, wg, NT), dot(n2, wu, NT), dot(c, wd, NT)
    sig = jax.nn.sigmoid(gate)
    silu = gate * sig
    z = (silu * up).astype(jnp.bfloat16)
    dg = (dz * up * (sig * (1.0 + gate * (1.0 - sig)))).astype(jnp.bfloat16)
    du = (dz * silu).astype(jnp.bfloat16)
    z_ref[0] = z
    g_ref[0] = dg
    u_ref[0] = du
    f_ref[0] = dot(z, wd, NN).astype(jnp.bfloat16)
    d_ref[0] = (dot(dg, wg, NN) + dot(du, wu, NN)).astype(jnp.bfloat16)


def ffn(n2, c, weights, hid):
    nb, rows, width = n2.shape
    n_t = weights.shape[0]
    total = n_t * hid
    bf = jnp.bfloat16
    full = pl.BlockSpec((1, rows, width), lambda s: (s, 0, 0))
    col = pl.BlockSpec((1, rows, total), lambda s: (s, 0, 0))
    kinds = [
        pl.BlockSpec(
            (n_t, hid, width),
            functools.partial(lambda which, s: (0, which, 0), which),
            pipeline_mode=pl.Buffered(1),
        )
        for which in range(3)
    ]
    return pl.pallas_call(
        ffn_kernel,
        name="ffn",
        grid=(nb,),
        out_shape=[jax.ShapeDtypeStruct((nb, rows, width), bf)] * 2
        + [jax.ShapeDtypeStruct((nb, rows, total), bf)] * 3,
        in_specs=[full] * 2 + kinds,
        out_specs=[full] * 2 + [col] * 3,
        compiler_params=pltpu.CompilerParams(vmem_limit_bytes=56 << 20),
        cost_estimate=pl.CostEstimate(
            flops=2 * nb * rows * width * total * 6,
            bytes_accessed=20 * 10**6,
            transcendentals=nb * rows * total,
        ),
    )(n2, c, weights, weights, weights)


def ffn_grad_kernel(nb, *refs):
    ns, cs, zs, gs, us = (refs[k * nb : (k + 1) * nb] for k in range(5))
    out = refs[5 * nb]
    pieces, rows, width = out.shape
    hid = rows // 3
    for which, (left, right) in enumerate(((gs, ns), (us, ns), (zs, cs))):
        total = dot(left[0][...], right[0][...], TN)
        for b in range(1, nb):
            total += dot(left[b][...], right[b][...], TN)
        out[:, which * hid : (which + 1) * hid] = total.astype(jnp.bfloat16).reshape(pieces, hid, width)


def ffn_grad(ns, cs, zs, gs, us, n_t):
    nb = len(ns)
    width = ns[0].shape[1]
    total = zs[0].shape[1]
    hid = total // n_t
    rows = sum(n.shape[0] for n in ns)
    full = [pl.BlockSpec(n.shape, lambda s: (0, 0)) for n in ns]
    col = [pl.BlockSpec((n.shape[0], HT), lambda s: (0, s)) for n in ns]
    return pl.pallas_call(
        functools.partial(ffn_grad_kernel, nb),
        name="ffn_grad",
        grid=(total // HT,),
        out_shape=jax.ShapeDtypeStruct((n_t, 3 * hid, width), jnp.bfloat16),
        in_specs=full * 2 + col * 3,
        out_specs=pl.BlockSpec((HT // hid, 3 * hid, width), lambda s: (s, 0, 0)),
        compiler_params=pltpu.CompilerParams(vmem_limit_bytes=56 << 20),
        cost_estimate=pl.CostEstimate(
            flops=2 * rows * width * total * 3, bytes_accessed=20 * 10**6, transcendentals=0
        ),
    )(*ns, *cs, *zs, *gs, *us)


def late_kernel(near, order_ref, gq_ref, all_ref, w_ref, gains_ref, heads_ref, gm_ref, keep_ref, send_ref):
    wide = gq_ref.shape[1]
    grads = dot(gq_ref[...], all_ref[...], TN)
    first = jnp.sum(grads * w_ref[...].astype(jnp.float32), axis=0, keepdims=True) / gains_ref[0:1]
    row = lax.broadcasted_iota(jnp.int32, (16, first.shape[1]), 0)
    gains = jnp.where(row == 0, first, jnp.where(row == 1, gains_ref[1:2], 0.0))
    outs = dot(heads_ref[...], gm_ref[...], TN)
    step = pl.program_id(0)

    def write(ref, kind):
        ref[0:wide] = grads.astype(kind)
        ref[wide : wide + 16] = gains.astype(kind)
        ref[wide + 16 :] = outs.astype(kind)

    @pl.when(step < near)
    def _():
        write(keep_ref, jnp.float32)

    @pl.when(step >= near)
    def _():
        write(send_ref, jnp.bfloat16)


def late_grads(order, grad_qkv, all1, w_qkv, gains, heads_own, grad_bf):
    n = order.shape[0]
    near = n // 2
    width = all1.shape[1]
    part = width // n
    whole = lambda x: pl.BlockSpec(x.shape, lambda i, o: (0, 0))
    block = lambda x: pl.BlockSpec((x.shape[0], part), lambda i, o: (0, o[i]))
    total = grad_qkv.shape[1] + 16 + heads_own.shape[1]
    return pl.pallas_call(
        functools.partial(late_kernel, near),
        name="late_grads",
        out_shape=(
            jax.ShapeDtypeStruct((total, near * part), jnp.float32),
            jax.ShapeDtypeStruct((total, near * part), jnp.bfloat16),
        ),
        grid_spec=pltpu.PrefetchScalarGridSpec(
            num_scalar_prefetch=1,
            grid=(n,),
            in_specs=[whole(grad_qkv), block(all1), block(w_qkv), block(gains), whole(heads_own), block(grad_bf)],
            out_specs=[
                pl.BlockSpec((total, part), lambda i, o: (0, jnp.minimum(i, near - 1))),
                pl.BlockSpec((total, part), lambda i, o: (0, jnp.maximum(i - near, 0))),
            ],
        ),
        compiler_params=pltpu.CompilerParams(vmem_limit_bytes=40 << 20),
        cost_estimate=pl.CostEstimate(flops=4 * 10**9, bytes_accessed=14 * 10**6, transcendentals=0),
    )(order, grad_qkv, all1, w_qkv, gains, heads_own, grad_bf)


def blank(shape, dtype):
    return pl.pallas_call(
        lambda out_ref: None,
        name="blank",
        out_shape=jax.ShapeDtypeStruct(shape, dtype),
        out_specs=pl.BlockSpec(memory_space=pl.ANY),
    )()


def row_scale(values):
    return lax.rsqrt(jnp.mean(values * values, axis=-1, keepdims=True) + EPS)


def norm_back(grad_normed, values, scale, gain):
    weighted = grad_normed * gain
    inner = jnp.mean(weighted * values, axis=-1, keepdims=True)
    return scale * weighted - values * (scale * scale * scale) * inner


def after(value, *others):
    return lax.optimization_barrier((value,) + others)[0]


def make(n_dp, n_t):
    ring = list(range(0, n_t, 2)) + list(range(n_t - 1, 0, -2))
    bf = jnp.bfloat16
    f32 = jnp.float32

    def hop(value, k):
        return lax.ppermute(value, "tensor", [(ring[i], ring[(i + k) % n_t]) for i in range(n_t)])

    def flip(value, k):
        return lax.ppermute(value, "dp", [(i, i ^ k) for i in range(n_dp)])

    def flip_t(value, k):
        return lax.ppermute(value, "tensor", [(i, i ^ k) for i in range(n_t)])

    bits = [1 << b for b in range(n_dp.bit_length() - 1)]
    t_bits = [1 << b for b in range(n_t.bit_length() - 2, -1, -1)]
    n_ff = min(n_dp, 4)
    ff_bits = [b for b in bits if b < n_ff]
    put = lax.dynamic_update_slice_in_dim
    take = lax.dynamic_slice_in_dim

    def pick(value, index, axis):
        return lax.dynamic_index_in_dim(value, index, axis, keepdims=False)

    dp_order = [0]
    for bit in bits[::-1]:
        dp_order = dp_order + [k ^ bit for k in dp_order]

    def arrange(value, me):
        size = value.shape[-1] // n_dp
        axis = value.ndim - 1
        return jnp.concatenate([take(value, (me ^ k) * size, size, axis) for k in dp_order], axis=axis)

    def scatter_sum_dp(arranged, send_type):
        for bit in bits:
            cut = arranged.shape[-1] // 2
            arranged = arranged[..., :cut] + flip(arranged[..., cut:].astype(send_type), bit).astype(f32)
        return arranged

    def scatter_sum_t(value, t, send_type):
        for bit in t_bits:
            halves = value.reshape((2, -1) + value.shape[1:])
            side = (t // bit) % 2
            value = pick(halves, side, 0) + flip_t(pick(halves, 1 - side, 0).astype(send_type), bit).astype(f32)
        return value[0]

    def on_device(
        tokens, seq_ids, blk_ids, norm1_gain, w_query, w_key, w_value, w_out, norm2_gain,
        w_gate, w_up, w_down, cotangent,
    ):
        d = lax.axis_index("dp")
        t = lax.axis_index("tensor")
        half_t = n_t // 2
        pos = jnp.where(t % 2 == 0, t // 2, n_t - 1 - t // 2)

        def owner(p):
            p = lax.rem(p + 2 * n_t, n_t)
            return jnp.where(p < half_t, 2 * p, 2 * (n_t - 1 - p) + 1)

        ahead = [owner(pos + j) for j in range(n_t)]
        behind = [owner(pos - j) for j in range(n_t)]
        own_rows, width = tokens.shape
        rows = own_rows * n_t
        half = own_rows // 2
        part = width // n_dp
        wide = w_query.shape[1]

        one, two = [tokens[:half]], [tokens[half:]]
        for k in range(1, n_t):
            one.append(hop(one[-1], 1))
            two.append(hop(two[-1], -1))

        def gather_dp(piece):
            whole = put(jnp.zeros((piece.shape[0], width), bf), piece, d * part, 1)
            for k in range(1, n_dp):
                whole = put(whole, flip(piece, k), (d ^ k) * part, 1)
            return whole

        common = gather_dp(
            jnp.concatenate(
                [
                    jnp.concatenate([w_query, w_key, w_value], axis=1).T,
                    norm1_gain[None],
                    norm2_gain[None],
                    jnp.zeros((14, part), bf),
                ]
            )
        )
        w_qkv = common[: 3 * wide]
        gains = common[3 * wide :].astype(f32)
        gain1, gain2 = gains[0:1], gains[1:2]

        hid_t = w_down.shape[0]
        hid = hid_t // n_ff
        out_half = wide // 2
        core = d % 2
        shards = jnp.concatenate(
            [
                w_gate.T.reshape(n_ff, hid, part),
                w_up.T.reshape(n_ff, hid, part),
                w_down.reshape(n_ff, hid, part),
                jnp.tile(w_out.reshape(2, out_half, part), (n_ff // 2, 1, 1)),
            ],
            axis=1,
        )
        shards = after(shards, one[1])
        pieces = [pick(shards, (d ^ k) % n_ff, 0) for k in range(n_dp)]
        pieces = [flip(piece, k) if k else piece for k, piece in enumerate(pieces)]
        pieces = lax.optimization_barrier((*pieces, one[WEIGHTS_AT], two[WEIGHTS_AT]))[:n_dp]
        own_w = jnp.zeros((3 * hid + out_half, width), bf)
        for k in range(n_dp):
            own_w = put(own_w, pieces[k], (d ^ k) * part, 1)
        own_o = own_w[3 * hid :]
        own_w = after(own_w[: 3 * hid], one[BULK_AT], two[BULK_AT])

        cot_far = cotangent[None]
        for bit in ff_bits[:0:-1]:
            cot_far = jnp.concatenate([cot_far, flip(after(cot_far, one[2]), bit)])

        resid = tokens.astype(f32)
        scale1 = row_scale(resid)

        def normed(piece):
            value = piece.astype(f32)
            return (value * row_scale(value) * gain1).astype(bf)

        def project(piece):
            return lax.dot_general(piece, w_qkv, NT, preferred_element_type=f32).astype(bf)

        mine = normed(tokens)
        all1 = put(blank((rows, width), bf), mine, t * own_rows, 0)
        qkv = put(blank((rows, 3 * wide), bf), project(mine), t * own_rows, 0)
        for k in range(1, n_t):
            both = normed(jnp.concatenate([one[k], two[k]]))
            made = project(both)
            all1 = put(all1, both[:half], behind[k] * own_rows, 0)
            all1 = put(all1, both[half:], ahead[k] * own_rows + half, 0)
            qkv = put(qkv, made[:half], behind[k] * own_rows, 0)
            qkv = put(qkv, made[half:], ahead[k] * own_rows + half, 0)

        o_mine = lax.all_gather(own_o, "tensor", axis=0)
        weights = lax.all_gather(own_w, "tensor", axis=0)
        o_mine = after(o_mine, qkv)
        o_peer = flip(o_mine, 1)
        out_full = jnp.where(
            core == 0,
            jnp.concatenate([o_mine, o_peer], axis=1),
            jnp.concatenate([o_peer, o_mine], axis=1),
        ).reshape(n_t * wide, width)
        cot_far = after(cot_far, qkv)
        c_near = jnp.concatenate([cotangent[None], flip(cot_far[:1], 1)])
        c_far = jnp.concatenate([cot_far[1:], flip(cot_far[1:], 1)])

        units = seq_ids.reshape(-1, 4 * BLK)[:, 0]
        n_units = rows // (4 * BLK)
        same = units[:, None] == units[None, :]
        first_unit = jnp.min(jnp.where(same, jnp.arange(n_units)[None, :], n_units), axis=1)
        first = jnp.repeat(first_unit * 4, 4).astype(jnp.int32)
        attended, logs = attn_fwd(qkv, first)

        heads_own = put(
            blank((own_rows, n_t * wide), bf), take(attended, t * own_rows, own_rows, 0), t * wide, 1
        )
        for j in range(1, n_t):
            piece = hop(take(attended, behind[j] * own_rows, own_rows, 0), -j)
            heads_own = put(heads_own, piece, ahead[j] * wide, 1)
        mixed = resid + jnp.dot(heads_own, out_full, preferred_element_type=f32)
        scale2 = row_scale(mixed)
        normed2 = (mixed * scale2 * gain2).astype(bf)

        n_far = normed2[None]
        for bit in ff_bits[:0:-1]:
            n_far = jnp.concatenate([n_far, flip(n_far, bit)])
        n_near = jnp.concatenate([normed2[None], flip(normed2[None], 1)])
        f_near, d_near, z_near, g_near, u_near = ffn(n_near, c_near, weights, hid)
        n_far = after(n_far[1:], d_near)
        n_far = jnp.concatenate([n_far, flip(n_far, 1)])
        f_far, d_far, z_far, g_far, u_far = ffn(n_far, c_far, weights, hid)

        def fold_core(near, far):
            cut = far.shape[0] // 2
            far_sum = far[:cut].astype(f32) + flip(far[cut:], 1).astype(f32)
            near_sum = near[:1].astype(f32) + flip(near[1:], 1).astype(f32)
            return jnp.concatenate([near_sum, far_sum])

        def fold_far(acc, *late):
            for bit in ff_bits[1:]:
                cut = acc.shape[0] // 2
                got = flip(acc[cut:].astype(bf), bit)
                acc = acc[:cut] + (after(got, *late) if bit == ff_bits[-1] else got).astype(f32)
            return acc[0]

        grad_w = ffn_grad(
            [n_near.reshape(-1, width), n_far.reshape(-1, width)],
            [c_near.reshape(-1, width), c_far.reshape(-1, width)],
            [z.reshape(-1, z.shape[-1]) for z in (z_near, z_far)],
            [g.reshape(-1, g.shape[-1]) for g in (g_near, g_far)],
            [u.reshape(-1, u.shape[-1]) for u in (u_near, u_far)],
            n_t,
        )
        grad_normed2 = fold_far(fold_core(d_near, d_far), grad_w)

        cot = cotangent.astype(f32)
        grad_mixed = cot + norm_back(grad_normed2, mixed, scale2, gain2)
        grad_bf = grad_mixed.astype(bf)
        grad_heads = lax.dot_general(grad_bf, out_full, NT, preferred_element_type=f32).astype(bf)
        grad_att = put(
            blank((rows, wide), bf), take(grad_heads, t * wide, wide, 1), t * own_rows, 0
        )
        for j in range(1, n_t):
            piece = hop(take(grad_heads, ahead[j] * wide, wide, 1), j)
            grad_att = put(grad_att, piece, behind[j] * own_rows, 0)
        f_folded = after(fold_core(f_near, f_far), grad_heads)
        grad_qkv = attn_bwd(qkv, grad_att, attended, logs, first)
        output = (mixed + fold_far(f_folded, grad_qkv)).astype(bf)
        summed = lax.psum_scatter(
            (after(grad_w, grad_att) if RS_LATE else grad_w).reshape(-1, width),
            "tensor", scatter_dimension=0, tiled=True,
        )

        def back_rows(k):
            pair = jnp.concatenate(
                [
                    take(grad_qkv, behind[k] * own_rows, half, 0),
                    take(grad_qkv, ahead[k] * own_rows + half, half, 0),
                ]
            )
            made = jnp.dot(pair, w_qkv, preferred_element_type=f32)
            return lax.optimization_barrier(made.astype(bf))

        made = back_rows(n_t - 1)
        up, down = [made[:half]], [made[half:]]
        for k in range(n_t - 2, -1, -1):
            got_up, got_down = hop(up[-1], -1), hop(down[-1], 1)
            made = back_rows(k).astype(f32)
            up.append(got_up.astype(f32) + made[:half])
            down.append(got_down.astype(f32) + made[half:])
            if k:
                up[-1], down[-1] = up[-1].astype(bf), down[-1].astype(bf)
        grad_normed1 = jnp.concatenate([up[-1], down[-1]])
        input_grad = (grad_mixed + norm_back(grad_normed1, resid, scale1, gain1)).astype(bf)

        grad_gain2 = jnp.sum(grad_normed2 * mixed * scale2, axis=0, keepdims=True)
        gain_rows = jnp.concatenate([gain1, grad_gain2, jnp.zeros((6, width), f32)])
        if part % 128 == 0:
            order = jnp.stack([d ^ k for k in dp_order]).astype(jnp.int32)
            keep, send = late_grads(order, grad_qkv, all1, w_qkv, gain_rows, heads_own, grad_bf)
        else:
            grad_wqkv = lax.dot_general(grad_qkv, all1, TN, preferred_element_type=f32)
            grad_gain1 = jnp.sum(grad_wqkv * w_qkv.astype(f32), axis=0, keepdims=True) / gain1
            grad_wo = lax.dot_general(heads_own, grad_bf, TN, preferred_element_type=f32)
            gain_rows = jnp.concatenate([grad_gain1, grad_gain2, jnp.zeros((14, width), f32)])
            both = arrange(jnp.concatenate([grad_wqkv, gain_rows, grad_wo]), d)
            keep, send = both[:, : width // 2], both[:, width // 2 :].astype(bf)
        stage = 1
        for bit in bits:
            send = after(send, up[min(stage, n_t - 2)])
            got = after(flip(send, bit), up[min(stage + 1, n_t - 2)])
            stage += 1 if bit == 1 else 2
            keep = keep + got.astype(f32)
            cut = keep.shape[1] // 2
            if cut >= part:
                keep, send = keep[:, :cut], keep[:, cut:].astype(bf)
        grad_query, grad_key, grad_value = (keep[k * wide : (k + 1) * wide].T for k in range(3))
        gain_sums = jnp.broadcast_to(keep[3 * wide : 3 * wide + 16], (n_t, 16, part))
        parts = jnp.concatenate([keep[3 * wide + 16 :].reshape(n_t, wide, part), gain_sums], axis=1)
        mine = scatter_sum_t(parts, t, bf)
        grad_out = mine[:wide]
        share = part // n_t
        grad_norm1 = take(mine[wide], t * share, share, 0)
        grad_norm2 = take(mine[wide + 1], t * share, share, 0)

        summed = after(summed, up[2]).reshape(3, hid, n_dp, part)
        full = blank((3, n_ff, hid, part), f32)
        for k in range(n_ff):
            total = 0.0
            for far in range(k, n_dp, n_ff):
                piece = pick(summed, d ^ far, 2)[:, None]
                piece = after(flip(piece, far), up[5]) if far else piece
                total = total + piece.astype(f32)
            full = put(full, total, (d ^ k) % n_ff, 1)
        full = full.reshape(3, hid_t, part)

        return (
            output, input_grad, grad_query, grad_key, grad_value, grad_out,
            full[0].T, full[1].T, full[2], grad_norm1, grad_norm2,
        )

    return on_device


def solution(mesh):
    rows = P(("dp", "tensor"), None)
    return jax.shard_map(
        make(mesh.shape["dp"], mesh.shape["tensor"]),
        mesh=mesh,
        in_specs=(
            rows, P("dp"), P("dp"), P("dp"), P("dp", "tensor"), P("dp", "tensor"),
            P("dp", "tensor"), P("tensor", "dp"), P("dp"), P("dp", "tensor"),
            P("dp", "tensor"), P("tensor", "dp"), rows,
        ),
        out_specs=(
            rows, rows, P("dp", "tensor"), P("dp", "tensor"), P("dp", "tensor"),
            P("tensor", "dp"), P("dp", "tensor"), P("dp", "tensor"), P("tensor", "dp"),
            P(("dp", "tensor")), P(("dp", "tensor")),
        ),
        check_vma=False,
    )
```

```python
import functools
import math

import jax
import jax.numpy as jnp
from jax import lax
from jax.experimental import pallas as pl
from jax.experimental.pallas import tpu as pltpu
from jax.sharding import PartitionSpec as P

DH = 64
BLK = 256
EPS = 1e-06
HT = 256
BULK_AT = 5
WEIGHTS_AT = 3
FOLD_AT = 2
FAR_AT = 4
FIRST_AT = 1
SPREAD_AT = 6
COMMON_AT = 4
COT_AT = 5
NT = (((1,), (1,)), ((), ()))
NN = (((1,), (0,)), ((), ()))
TN = (((0,), (0,)), ((), ()))


def dot(a, b, dims):
    return lax.dot_general(a, b, dims, preferred_element_type=jnp.float32)


def split_heads(block):
    low = lax.broadcasted_iota(jnp.int32, block.shape, 1) < DH
    zero = jnp.zeros_like(block)
    return jnp.concatenate([jnp.where(low, block, zero), jnp.where(low, zero, block)], axis=0)


def scaled_q(qkv_ref, rows):
    return split_heads((qkv_ref[rows, 0:128].astype(jnp.float32) * DH ** -0.5).astype(jnp.bfloat16))


def in_pairs(first, last, ahead, work):
    count = last - first + 1
    ahead(first, 0)

    def pair(p, _):
        j = first + 2 * p
        ahead(j + 1, 1)
        work(j, 0)
        ahead(jnp.minimum(j + 2, last), 0)
        work(j + 1, 1)
        return 0

    lax.fori_loop(0, count // 2, pair, 0)

    @pl.when(count % 2 == 1)
    def _():
        work(last, 0)


def attn_fwd_kernel(first_ref, qkv_ref, out_ref, log_ref, vt_ref, top_ref, sum_ref, acc_ref, qt_ref, *score_refs):
    i = pl.program_id(0)
    @pl.when(i == 0)
    def _():
        vt_ref[...] = jnp.transpose(qkv_ref[:, 256:384])
    rows = pl.ds(pl.multiple_of(i * BLK, BLK), BLK)
    qt_ref[...] = jnp.transpose(scaled_q(qkv_ref, rows))
    top_ref[...] = jnp.full_like(top_ref, -1e30)
    sum_ref[...] = jnp.zeros_like(sum_ref)
    acc_ref[...] = jnp.zeros_like(acc_ref)

    def ahead(j, slot):
        at = pl.ds(pl.multiple_of(j * BLK, BLK), BLK)
        score_refs[slot][...] = dot(qkv_ref[at, 128:256], qt_ref[...], NN)

    def work(j, slot):
        at = pl.ds(pl.multiple_of(j * BLK, BLK), BLK)
        scores = score_refs[slot][...]
        old = top_ref[...]
        new = jnp.maximum(old, jnp.max(scores, axis=0, keepdims=True))
        top_ref[...] = new
        weights = jnp.exp(scores - new)
        shrink = jnp.exp(old - new)
        sum_ref[...] = sum_ref[...] * shrink + jnp.sum(weights, axis=0, keepdims=True)
        probs = weights.astype(jnp.bfloat16)
        acc_ref[:, 0:BLK] = acc_ref[:, 0:BLK] * shrink[:, 0:BLK] + dot(vt_ref[0:DH, at], probs[:, 0:BLK], NN)
        acc_ref[:, BLK:] = acc_ref[:, BLK:] * shrink[:, BLK:] + dot(vt_ref[DH:, at], probs[:, BLK:], NN)

    in_pairs(first_ref[i], i, ahead, work)
    mixed = acc_ref[...] / sum_ref[...]
    out_ref[...] = jnp.transpose(jnp.concatenate([mixed[:, 0:BLK], mixed[:, BLK:]], axis=0)).astype(jnp.bfloat16)
    log_ref[0] = top_ref[...] + jnp.log(sum_ref[...])


def attn_fwd(qkv, first):
    rows = qkv.shape[0]
    n = rows // BLK
    f32 = jnp.float32
    return pl.pallas_call(
        attn_fwd_kernel, name="attn_fwd",
        out_shape=(jax.ShapeDtypeStruct((rows,128),jnp.bfloat16), jax.ShapeDtypeStruct((n,1,2*BLK),f32)),
        grid_spec=pltpu.PrefetchScalarGridSpec(
            num_scalar_prefetch=1, grid=(n,),
            in_specs=[pl.BlockSpec((rows,384), lambda i,s:(0,0))],
            out_specs=[pl.BlockSpec((BLK,128), lambda i,s:(i,0)), pl.BlockSpec((1,1,2*BLK), lambda i,s:(i,0,0))],
            scratch_shapes=[pltpu.VMEM((128,rows),jnp.bfloat16), pltpu.VMEM((1,2*BLK),f32), pltpu.VMEM((1,2*BLK),f32), pltpu.VMEM((DH,2*BLK),f32),pltpu.VMEM((128,2*BLK),jnp.bfloat16)]+[pltpu.VMEM((BLK,2*BLK),f32)]*2),
        compiler_params=pltpu.CompilerParams(vmem_limit_bytes=32<<20),
        cost_estimate=pl.CostEstimate(flops=1000, bytes_accessed=1000, transcendentals=0),
    )(first, qkv)


def attn_bwd_kernel(first_ref, qkv_ref, do_ref, o_ref, log_ref, out_ref, kt_ref, dk_ref, dv_ref, dq_ref, qt_ref, gt_ref, *score_refs):
    i = pl.program_id(0)
    @pl.when(i == 0)
    def _():
        kt_ref[...] = jnp.transpose(qkv_ref[:, 128:256])
        dk_ref[...] = jnp.zeros_like(dk_ref)
        dv_ref[...] = jnp.zeros_like(dv_ref)
    rows = pl.ds(pl.multiple_of(i * BLK, BLK), BLK)
    both = scaled_q(qkv_ref, rows)
    grads = split_heads(do_ref[...])
    logs = log_ref[0]
    qt_ref[...] = jnp.transpose(both)
    turned = jnp.transpose(grads)
    gt_ref[...] = turned
    outs = jnp.transpose(o_ref[...]).astype(jnp.float32)
    delta = jnp.sum(turned.astype(jnp.float32) * jnp.concatenate([outs, outs], axis=1), axis=0, keepdims=True)
    dq_ref[...] = jnp.zeros_like(dq_ref)

    def ahead(j, slot):
        at = pl.ds(pl.multiple_of(j * BLK, BLK), BLK)
        score_refs[slot][...] = dot(qkv_ref[at, 128:256], qt_ref[...], NN)
        score_refs[2 + slot][...] = dot(qkv_ref[at, 256:384], gt_ref[...], NN)

    def work(j, slot):
        at = pl.ds(pl.multiple_of(j * BLK, BLK), BLK)
        probs = jnp.exp(score_refs[slot][...] - logs)
        ds = (probs * (score_refs[2 + slot][...] - delta)).astype(jnp.bfloat16)
        dv_ref[at, :] += dot(probs.astype(jnp.bfloat16), grads, NN)
        dk_ref[at, :] += dot(ds, both, NN)
        dq_ref[:, 0:BLK] += dot(kt_ref[0:DH, at], ds[:, 0:BLK], NN)
        dq_ref[:, BLK:] += dot(kt_ref[DH:, at], ds[:, BLK:], NN)

    in_pairs(first_ref[i], i, ahead, work)
    dq = jnp.concatenate([dq_ref[:, 0:BLK], dq_ref[:, BLK:]], axis=0)
    out_ref[rows, 0:128] = (jnp.transpose(dq) * DH ** -0.5).astype(jnp.bfloat16)

    @pl.when(i == pl.num_programs(0) - 1)
    def _():
        out_ref[:, 128:256] = dk_ref[...].astype(jnp.bfloat16)
        out_ref[:, 256:384] = dv_ref[...].astype(jnp.bfloat16)


def attn_bwd(qkv, do, o, log, first):
    rows = qkv.shape[0]
    n = rows // BLK
    f32 = jnp.float32
    blk = pl.BlockSpec((BLK,128), lambda i,s:(i,0))
    return pl.pallas_call(
        attn_bwd_kernel, name="attn_bwd",
        out_shape=jax.ShapeDtypeStruct((rows,384),jnp.bfloat16),
        grid_spec=pltpu.PrefetchScalarGridSpec(
            num_scalar_prefetch=1, grid=(n,),
            in_specs=[pl.BlockSpec((rows,384), lambda i,s:(0,0)), blk, blk, pl.BlockSpec((1,1,2*BLK), lambda i,s:(i,0,0))],
            out_specs=pl.BlockSpec((rows,384), lambda i,s:(0,0)),
            scratch_shapes=[pltpu.VMEM((128,rows),jnp.bfloat16), pltpu.VMEM((rows,128),f32), pltpu.VMEM((rows,128),f32), pltpu.VMEM((DH,2*BLK),f32)]+[pltpu.VMEM((128,2*BLK),jnp.bfloat16)]*2+[pltpu.VMEM((BLK,2*BLK),f32)]*4),
        compiler_params=pltpu.CompilerParams(vmem_limit_bytes=40<<20),
        cost_estimate=pl.CostEstimate(flops=1000, bytes_accessed=1000, transcendentals=0),
    )(first, qkv, do, o, log)


def ffn_kernel(nb, *refs):
    ns, cs = refs[:nb], refs[nb : 2 * nb]
    gate_ref, up_ref, down_ref = refs[2 * nb : 2 * nb + 3]
    f_ref, d_ref, z_ref, g_ref, u_ref, n_ref, c_ref = refs[-7:]
    before = refs[2 * nb + 3 : -7]
    for b in range(nb):

        @pl.when(pl.program_id(0) == b)
        def _():
            n_ref[...] = ns[b][...]
            c_ref[...] = cs[b][...]

    n2, c = n_ref[...], c_ref[...]
    wg, wu, wd = (ref[...].reshape(-1, n2.shape[1]) for ref in (gate_ref, up_ref, down_ref))
    gate, up, dz = dot(n2, wg, NT), dot(n2, wu, NT), dot(c, wd, NT)
    sig = jax.nn.sigmoid(gate)
    silu = gate * sig
    z = (silu * up).astype(jnp.bfloat16)
    dg = (dz * up * (sig * (1.0 + gate * (1.0 - sig)))).astype(jnp.bfloat16)
    du = (dz * silu).astype(jnp.bfloat16)
    z_ref[0] = z
    g_ref[0] = dg
    u_ref[0] = du
    f, d = dot(z, wd, NN), dot(dg, wg, NN) + dot(du, wu, NN)
    if before:
        f += before[0][0].astype(jnp.float32)
        d += before[1][0].astype(jnp.float32)
    f_ref[0] = f.astype(jnp.bfloat16)
    d_ref[0] = d.astype(jnp.bfloat16)


def ffn(ns, cs, weights, hid, before=()):
    nb = len(ns)
    rows, width = ns[0].shape
    n_t = weights.shape[0]
    total = n_t * hid
    bf = jnp.bfloat16
    full = pl.BlockSpec((1, rows, width), lambda s: (s, 0, 0))
    whole = pl.BlockSpec((rows, width), lambda s: (0, 0))
    col = pl.BlockSpec((1, rows, total), lambda s: (s, 0, 0))
    kinds = [
        pl.BlockSpec(
            (n_t, hid, width),
            functools.partial(lambda which, s: (0, which, 0), which),
            pipeline_mode=pl.Buffered(1),
        )
        for which in range(3)
    ]
    return pl.pallas_call(
        functools.partial(ffn_kernel, nb),
        name="ffn",
        grid=(nb,),
        out_shape=[jax.ShapeDtypeStruct((nb, rows, width), bf)] * 2
        + [jax.ShapeDtypeStruct((nb, rows, total), bf)] * 3,
        in_specs=[whole] * (2 * nb) + kinds + [full] * len(before),
        out_specs=[full] * 2 + [col] * 3,
        scratch_shapes=[pltpu.VMEM((rows, width), bf)] * 2,
        compiler_params=pltpu.CompilerParams(vmem_limit_bytes=56 << 20),
        cost_estimate=pl.CostEstimate(flops=1000, bytes_accessed=1000, transcendentals=0),
    )(*ns, *cs, weights, weights, weights, *before)


def ffn_grad_kernel(nb, calls, *refs):
    ns, cs = refs[:nb], refs[nb : 2 * nb]
    zs, gs, us = (refs[2 * nb + k * calls : 2 * nb + (k + 1) * calls] for k in range(3))
    out, n_ref, c_ref = refs[-3:]
    pieces, rows, width = out.shape
    hid = rows // 3
    own_rows = ns[0].shape[0]

    @pl.when(pl.program_id(0) == 0)
    def _():
        for b in range(nb):
            n_ref[b * own_rows : (b + 1) * own_rows] = ns[b][...]
            c_ref[b * own_rows : (b + 1) * own_rows] = cs[b][...]

    for which, (left, right) in enumerate(((gs, n_ref), (us, n_ref), (zs, c_ref))):
        total, at = None, 0
        for ref in left:
            block = ref[...].reshape(-1, ref.shape[-1])
            made = dot(block, right[at : at + block.shape[0]], TN)
            total = made if total is None else total + made
            at += block.shape[0]
        out[:, which * hid : (which + 1) * hid] = total.astype(jnp.bfloat16).reshape(pieces, hid, width)


def ffn_grad(ns, cs, zs, gs, us, n_t):
    nb = len(ns)
    rows, width = ns[0].shape
    total = zs[0].shape[2]
    hid = total // n_t
    tile = hid if hid % 128 == 0 else hid * (128 // math.gcd(hid, 128))
    tile = tile * max(HT // tile, 1)
    full = [pl.BlockSpec((rows, width), lambda s: (0, 0), pipeline_mode=pl.Buffered(1))] * nb
    col = [pl.BlockSpec((z.shape[0], rows, tile), lambda s: (0, 0, s)) for z in zs]
    return pl.pallas_call(
        functools.partial(ffn_grad_kernel, nb, len(zs)),
        name="ffn_grad",
        grid=(total // tile,),
        out_shape=jax.ShapeDtypeStruct((n_t, 3 * hid, width), jnp.bfloat16),
        in_specs=full * 2 + col * 3,
        out_specs=pl.BlockSpec((tile // hid, 3 * hid, width), lambda s: (s, 0, 0)),
        scratch_shapes=[pltpu.VMEM((nb * rows, width), jnp.bfloat16)] * 2,
        compiler_params=pltpu.CompilerParams(vmem_limit_bytes=56 << 20),
        cost_estimate=pl.CostEstimate(flops=1000, bytes_accessed=1000, transcendentals=0),
    )(*ns, *cs, *zs, *gs, *us)


def late_kernel(near, order_ref, gq_ref, all_ref, w_ref, gains_ref, heads_ref, gm_ref, keep_ref, send_ref):
    wide = gq_ref.shape[1]
    grads = dot(gq_ref[...], all_ref[...], TN)
    first = jnp.sum(grads * w_ref[...].astype(jnp.float32), axis=0, keepdims=True) / gains_ref[0:1]
    row = lax.broadcasted_iota(jnp.int32, (16, first.shape[1]), 0)
    gains = jnp.where(row == 0, first, jnp.where(row == 1, gains_ref[1:2], 0.0))
    outs = dot(heads_ref[...], gm_ref[...], TN)
    step = pl.program_id(0)

    def write(ref, kind):
        ref[0:wide] = grads.astype(kind)
        ref[wide : wide + 16] = gains.astype(kind)
        ref[wide + 16 :] = outs.astype(kind)

    @pl.when(step < near)
    def _():
        write(keep_ref, jnp.float32)

    @pl.when(step >= near)
    def _():
        write(send_ref, jnp.bfloat16)


def late_grads(order, grad_qkv, all1, w_qkv, gains, heads_own, grad_bf):
    n = order.shape[0]
    near = n // 2
    width = all1.shape[1]
    part = width // n
    whole = lambda x: pl.BlockSpec(x.shape, lambda i, o: (0, 0))
    block = lambda x: pl.BlockSpec((x.shape[0], part), lambda i, o: (0, o[i]))
    total = grad_qkv.shape[1] + 16 + heads_own.shape[1]
    return pl.pallas_call(
        functools.partial(late_kernel, near),
        name="late_grads",
        out_shape=(
            jax.ShapeDtypeStruct((total, near * part), jnp.float32),
            jax.ShapeDtypeStruct((total, near * part), jnp.bfloat16),
        ),
        grid_spec=pltpu.PrefetchScalarGridSpec(
            num_scalar_prefetch=1,
            grid=(n,),
            in_specs=[whole(grad_qkv), block(all1), block(w_qkv), block(gains), whole(heads_own), block(grad_bf)],
            out_specs=[
                pl.BlockSpec((total, part), lambda i, o: (0, jnp.minimum(i, near - 1))),
                pl.BlockSpec((total, part), lambda i, o: (0, jnp.maximum(i - near, 0))),
            ],
        ),
        compiler_params=pltpu.CompilerParams(vmem_limit_bytes=40 << 20),
        cost_estimate=pl.CostEstimate(flops=1000, bytes_accessed=1000, transcendentals=0),
    )(order, grad_qkv, all1, w_qkv, gains, heads_own, grad_bf)


def arrive_kernel(order_ref, one_ref, two_ref, gains_ref, w_ref, *refs):
    all_ref, qkv_ref = refs[-2:]

    def work(source):
        value = source[...].astype(jnp.float32)
        scale = lax.rsqrt(jnp.mean(value * value, axis=-1, keepdims=True) + EPS)
        normed = (value * scale * gains_ref[0:1]).astype(jnp.bfloat16)
        all_ref[...] = normed
        qkv_ref[...] = dot(normed, w_ref[...], NT).astype(jnp.bfloat16)

    @pl.when(pl.program_id(0) == 0)
    def _():
        work(one_ref)

    @pl.when(pl.program_id(0) == 1)
    def _():
        work(two_ref)


def arrive(order, one, two, gains, w_qkv, rows, state):
    half, width = one.shape
    cols = w_qkv.shape[0]
    whole = lambda x: pl.BlockSpec(x.shape, lambda i, o: (0, 0))
    old = () if state is None else state
    return pl.pallas_call(
        arrive_kernel,
        name="arrive",
        out_shape=(
            pltpu.HBM((rows, width), jnp.bfloat16),
            pltpu.HBM((rows, cols), jnp.bfloat16),
        ),
        grid_spec=pltpu.PrefetchScalarGridSpec(
            num_scalar_prefetch=1,
            grid=(2,),
            in_specs=[whole(one), whole(two), whole(gains), whole(w_qkv)]
            + [pl.BlockSpec(memory_space=pltpu.HBM)] * len(old),
            out_specs=[
                pl.BlockSpec((half, width), lambda i, o: (o[i], 0)),
                pl.BlockSpec((half, cols), lambda i, o: (o[i], 0)),
            ],
        ),
        input_output_aliases={5 + k: k for k in range(len(old))},
        compiler_params=pltpu.CompilerParams(vmem_limit_bytes=24 << 20),
        cost_estimate=pl.CostEstimate(flops=1000, bytes_accessed=1000, transcendentals=0),
    )(order, one, two, gains, w_qkv, *old)


def join_kernel(pieces, order_ref, *refs):
    out_ref = refs[-1]
    for k in range(pieces):

        @pl.when(pl.program_id(0) == k)
        def _():
            out_ref[...] = refs[k][...]


def join(order, pieces):
    rows, part = pieces[0].shape
    n = len(pieces)
    return pl.pallas_call(
        functools.partial(join_kernel, n),
        name="join",
        out_shape=jax.ShapeDtypeStruct((rows, n * part), pieces[0].dtype),
        grid_spec=pltpu.PrefetchScalarGridSpec(
            num_scalar_prefetch=1,
            grid=(n,),
            in_specs=[pl.BlockSpec((rows, part), lambda i, o: (0, 0))] * n,
            out_specs=pl.BlockSpec((rows, part), lambda i, o: (0, o[i])),
        ),
        compiler_params=pltpu.CompilerParams(vmem_limit_bytes=16 << 20),
        cost_estimate=pl.CostEstimate(flops=1000, bytes_accessed=1000, transcendentals=0),
    )(order, *pieces)


def blank(shape, dtype):
    return pl.pallas_call(
        lambda out_ref: None,
        name="blank",
        out_shape=jax.ShapeDtypeStruct(shape, dtype),
        out_specs=pl.BlockSpec(memory_space=pl.ANY),
    )()


def row_scale(values):
    return lax.rsqrt(jnp.mean(values * values, axis=-1, keepdims=True) + EPS)


def norm_back(grad_normed, values, scale, gain):
    weighted = grad_normed * gain
    inner = jnp.mean(weighted * values, axis=-1, keepdims=True)
    return scale * weighted - values * (scale * scale * scale) * inner


def after(value, *others):
    return lax.optimization_barrier((value,) + others)[0]


def make(n_dp, n_t):
    ring = list(range(0, n_t, 2)) + list(range(n_t - 1, 0, -2))
    bf = jnp.bfloat16
    f32 = jnp.float32

    def hop(value, k):
        return lax.ppermute(value, "tensor", [(ring[i], ring[(i + k) % n_t]) for i in range(n_t)])

    def flip(value, k):
        return lax.ppermute(value, "dp", [(i, i ^ k) for i in range(n_dp)])

    def flip_t(value, k):
        return lax.ppermute(value, "tensor", [(i, i ^ k) for i in range(n_t)])

    bits = [1 << b for b in range(n_dp.bit_length() - 1)]
    t_bits = [1 << b for b in range(n_t.bit_length() - 1)]
    n_ff = min(n_dp, 4)
    ff_bits = [b for b in bits if b < n_ff]
    put = lax.dynamic_update_slice_in_dim
    take = lax.dynamic_slice_in_dim

    def pick(value, index, axis):
        return lax.dynamic_index_in_dim(value, index, axis, keepdims=False)

    dp_order = [0]
    for bit in bits[::-1]:
        dp_order = dp_order + [k ^ bit for k in dp_order]

    def arrange(value, me):
        size = value.shape[-1] // n_dp
        axis = value.ndim - 1
        return jnp.concatenate([take(value, (me ^ k) * size, size, axis) for k in dp_order], axis=axis)

    def scatter_sum_dp(arranged, send_type):
        for bit in bits:
            cut = arranged.shape[-1] // 2
            arranged = arranged[..., :cut] + flip(arranged[..., cut:].astype(send_type), bit).astype(f32)
        return arranged

    def fold_t(value, t, bit, send_type):
        halves = value.reshape((-1, 2) + value.shape[1:])
        side = (t // bit) % 2
        return pick(halves, side, 1) + flip_t(pick(halves, 1 - side, 1).astype(send_type), bit).astype(f32)

    def on_device(
        tokens, seq_ids, blk_ids, norm1_gain, w_query, w_key, w_value, w_out, norm2_gain,
        w_gate, w_up, w_down, cotangent,
    ):
        d = lax.axis_index("dp")
        t = lax.axis_index("tensor")
        half_t = n_t // 2
        pos = jnp.where(t % 2 == 0, t // 2, n_t - 1 - t // 2)

        def owner(p):
            p = lax.rem(p + 2 * n_t, n_t)
            return jnp.where(p < half_t, 2 * p, 2 * (n_t - 1 - p) + 1)

        ahead = [owner(pos + j) for j in range(n_t)]
        behind = [owner(pos - j) for j in range(n_t)]
        own_rows, width = tokens.shape
        rows = own_rows * n_t
        half = own_rows // 2
        part = width // n_dp
        wide = w_query.shape[1]

        def gather_dp(piece):
            whole = put(jnp.zeros((piece.shape[0], width), bf), piece, d * part, 1)
            for k in range(1, n_dp):
                whole = put(whole, flip(piece, k), (d ^ k) * part, 1)
            return whole

        common = gather_dp(
            jnp.concatenate(
                [
                    jnp.concatenate([w_query, w_key, w_value], axis=1).T,
                    norm1_gain[None],
                    norm2_gain[None],
                    jnp.zeros((14, part), bf),
                ]
            )
        )
        one, two = [tokens[:half]], [tokens[half:]]
        for k in range(1, n_t):
            got = [hop(one[-1], 1), hop(two[-1], -1)]
            if k == COMMON_AT:
                got[0], got[1], common = lax.optimization_barrier((*got, common))
            one.append(got[0])
            two.append(got[1])
        w_qkv = common[: 3 * wide]
        gains = common[3 * wide :].astype(f32)
        gain1, gain2 = gains[0:1], gains[1:2]

        hid_t = w_down.shape[0]
        hid = hid_t // n_ff
        out_half = wide // 2
        core = d % 2
        cuts = (hid * 3 // 4, hid - hid * 3 // 4)
        thirds = [w.reshape(n_ff, hid, part) for w in (w_gate.T, w_up.T, w_down)]
        shards = jnp.concatenate(
            [
                *(w[:, : cuts[0]] for w in thirds),
                *(w[:, cuts[0] :] for w in thirds),
                jnp.tile(w_out.reshape(2, out_half, part), (n_ff // 2, 1, 1)),
            ],
            axis=1,
        )
        shards = after(shards, one[1])
        pieces = [pick(shards, (d ^ k) % n_ff, 0) for k in range(n_dp)]
        pieces = [flip(piece, k) if k else piece for k, piece in enumerate(pieces)]
        pieces = lax.optimization_barrier((*pieces, one[WEIGHTS_AT], two[WEIGHTS_AT]))[:n_dp]
        own_w = jnp.zeros((3 * hid + out_half, width), bf)
        for k in range(n_dp):
            own_w = put(own_w, pieces[k], (d ^ k) * part, 1)
        own_o = own_w[3 * hid :]
        own_w = after(own_w[: 3 * hid], one[BULK_AT], two[BULK_AT])

        cot_far = cotangent[None]
        for bit in ff_bits[:0:-1]:
            cot_far = jnp.concatenate([cot_far, flip(after(cot_far, one[COT_AT]), bit)])

        resid = tokens.astype(f32)
        scale1 = row_scale(resid)

        def normed(piece):
            value = piece.astype(f32)
            return (value * row_scale(value) * gain1).astype(bf)

        def project(piece):
            return lax.dot_general(piece, w_qkv, NT, preferred_element_type=f32).astype(bf)

        mine = normed(tokens)
        all1 = put(blank((rows, width), bf), mine, t * own_rows, 0)
        qkv = put(blank((rows, 3 * wide), bf), project(mine), t * own_rows, 0)
        for k in range(1, n_t):
            both = normed(jnp.concatenate([one[k], two[k]]))
            made = project(both)
            all1 = put(all1, both[:half], behind[k] * own_rows, 0)
            all1 = put(all1, both[half:], ahead[k] * own_rows + half, 0)
            qkv = put(qkv, made[:half], behind[k] * own_rows, 0)
            qkv = put(qkv, made[half:], ahead[k] * own_rows + half, 0)

        o_mine = lax.all_gather(own_o, "tensor", axis=0)
        cut_w = 3 * cuts[0]
        weights = [lax.all_gather(piece, "tensor", axis=0) for piece in (own_w[:cut_w], own_w[cut_w:])]
        o_mine = after(o_mine, qkv)
        o_peer = flip(o_mine, 1)
        out_full = jnp.where(
            core == 0,
            jnp.concatenate([o_mine, o_peer], axis=1),
            jnp.concatenate([o_peer, o_mine], axis=1),
        ).reshape(n_t * wide, width)
        cot_far = after(cot_far, qkv)
        c_near = [cotangent, flip(cot_far[0], 1)]
        c_far = [cot_far[m] for m in range(1, n_ff // 2)]
        c_far += [flip(c, 1) for c in c_far]

        units = seq_ids.reshape(-1, 4 * BLK)[:, 0]
        n_units = rows // (4 * BLK)
        same = units[:, None] == units[None, :]
        first_unit = jnp.min(jnp.where(same, jnp.arange(n_units)[None, :], n_units), axis=1)
        first = jnp.repeat(first_unit * 4, 4).astype(jnp.int32)
        attended, logs = attn_fwd(qkv, first)

        heads_own = put(
            blank((own_rows, n_t * wide), bf), take(attended, t * own_rows, own_rows, 0), t * wide, 1
        )
        for j in range(1, n_t):
            piece = hop(take(attended, behind[j] * own_rows, own_rows, 0), -j)
            heads_own = put(heads_own, piece, ahead[j] * wide, 1)
        mixed = resid + jnp.dot(heads_own, out_full, preferred_element_type=f32)
        scale2 = row_scale(mixed)
        normed2 = (mixed * scale2 * gain2).astype(bf)
        normed2, all1 = lax.optimization_barrier((normed2, all1))

        n_far = normed2[None]
        for bit in ff_bits[:0:-1]:
            n_far = jnp.concatenate([n_far, flip(n_far, bit)])
        n_near = [normed2, flip(normed2, 1)]
        f_near, d_near, *left_near = ffn(n_near, c_near, weights[0], cuts[0])
        n_far = after(n_far[1:], d_near)
        n_far = [n_far[m] for m in range(n_ff // 2 - 1)]
        n_far += [flip(n, 1) for n in n_far]
        f_far, d_far, *left_far = ffn(n_far, c_far, weights[0], cuts[0])

        def grad_w(near, far):
            return ffn_grad(n_near + n_far, c_near + c_far, *zip(near, far), n_t)

        def sum_w(grads):
            return lax.psum_scatter(grads.reshape(-1, width), "tensor", scatter_dimension=0, tiled=True)

        first_w = grad_w(left_near, left_far)
        half_sums = [sum_w(first_w)]
        later_w = after(weights[1], first_w)
        f_near, d_near, *left_near = ffn(n_near, c_near, later_w, cuts[1], (f_near, d_near))
        f_far, d_far, *left_far = ffn(n_far, c_far, later_w, cuts[1], (f_far, d_far))

        def fold_core(near, far):
            cut = far.shape[0] // 2
            far_sum = far[:cut].astype(f32) + flip(far[cut:], 1).astype(f32)
            near_sum = near[:1].astype(f32) + flip(near[1:], 1).astype(f32)
            return near_sum, far_sum

        def fold_far(near_sum, far_sum, beside=None):
            acc = jnp.concatenate([near_sum, far_sum])
            made = None
            for bit in ff_bits[1:]:
                cut = acc.shape[0] // 2
                sent = acc[cut:].astype(bf)
                if beside is not None and bit == ff_bits[-1]:
                    sent, made = beside(sent)
                got = flip(sent, bit)
                if made is not None:
                    got = after(got, made)
                acc = acc[:cut] + got.astype(f32)
            return acc[0], made

        def grad_w_beside(sent):
            sent, *left = lax.optimization_barrier((sent, *left_near, *left_far))
            return sent, grad_w(left[:3], left[3:])

        grad_normed2, second_w = fold_far(*fold_core(d_near, d_far), grad_w_beside)
        half_sums.append(sum_w(after(second_w, grad_normed2)))

        cot = cotangent.astype(f32)
        grad_mixed = cot + norm_back(grad_normed2, mixed, scale2, gain2)
        grad_bf = grad_mixed.astype(bf)
        grad_heads = lax.dot_general(grad_bf, out_full, NT, preferred_element_type=f32).astype(bf)
        grad_att = put(
            blank((rows, wide), bf), take(grad_heads, t * wide, wide, 1), t * own_rows, 0
        )
        for j in range(1, n_t):
            piece = hop(take(grad_heads, ahead[j] * wide, wide, 1), j)
            grad_att = put(grad_att, piece, behind[j] * own_rows, 0)
        grad_qkv = attn_bwd(qkv, grad_att, attended, logs, first)
        def back_rows(k, *late):
            source = after(grad_qkv, *late)
            pair = jnp.concatenate(
                [
                    take(source, behind[k] * own_rows, half, 0),
                    take(source, ahead[k] * own_rows + half, half, 0),
                ]
            )
            made = jnp.dot(pair, w_qkv, preferred_element_type=f32)
            return lax.optimization_barrier(made.astype(bf))

        grad_gain2 = jnp.sum(grad_normed2 * mixed * scale2, axis=0, keepdims=True)
        gain_rows = jnp.concatenate([gain1, grad_gain2, jnp.zeros((6, width), f32)])

        def first_late(source):
            if part % 128 == 0:
                order = jnp.stack([d ^ k for k in dp_order]).astype(jnp.int32)
                return late_grads(order, source, all1, w_qkv, gain_rows, heads_own, grad_bf)
            grad_wqkv = lax.dot_general(source, all1, TN, preferred_element_type=f32)
            grad_gain1 = jnp.sum(grad_wqkv * w_qkv.astype(f32), axis=0, keepdims=True) / gain1
            grad_wo = lax.dot_general(heads_own, grad_bf, TN, preferred_element_type=f32)
            gain_grads = jnp.concatenate([grad_gain1, grad_gain2, jnp.zeros((14, width), f32)])
            both = arrange(jnp.concatenate([grad_wqkv, gain_grads, grad_wo]), d)
            return both[:, : width // 2], both[:, width // 2 :].astype(bf)

        def spread(summed):
            summed = jnp.concatenate(
                [m.reshape(3, -1, width) for m in summed], axis=1
            ).reshape(3, hid, n_dp, part)
            totals = []
            for k in range(n_ff):
                total = 0.0
                for far in range(k, n_dp, n_ff):
                    piece = pick(summed, d ^ far, 2)[:, None]
                    total = total + (flip(piece, far) if far else piece).astype(f32)
                totals.append(total)
            return totals

        made = back_rows(n_t - 1)
        up, down = [made[:half]], [made[half:]]
        keep = send = parts = got = None
        left = list(bits)
        tensor_left = list(t_bits)
        for step in range(1, n_t):
            k = n_t - 1 - step
            got_up, got_down = hop(up[-1], -1), hop(down[-1], 1)
            made = back_rows(k, up[max(step - 2, 0)]).astype(f32)
            new_up, new_down = got_up.astype(f32) + made[:half], got_down.astype(f32) + made[half:]
            if k:
                new_up, new_down = new_up.astype(bf), new_down.astype(bf)
            if step == 1:
                keep, send = first_late(grad_qkv)
                new_up, new_down, keep, send = lax.optimization_barrier((new_up, new_down, keep, send))
            elif left:
                bit = left[0]
                if got is None:
                    got = flip(send, bit)
                    wait = 0 if bit == 1 else 1
                else:
                    wait -= 1
                if wait == 0:
                    new_up, new_down, got = lax.optimization_barrier((new_up, new_down, got))
                    keep = keep + got.astype(f32)
                    cut = keep.shape[1] // 2
                    if cut >= part:
                        keep, send = keep[:, :cut], keep[:, cut:].astype(bf)
                    left.pop(0)
                    got = None
            elif tensor_left:
                if parts is None:
                    gain_sums = jnp.broadcast_to(keep[3 * wide : 3 * wide + 16], (n_t, 16, part))
                    parts = jnp.concatenate([keep[3 * wide + 16 :].reshape(n_t, wide, part), gain_sums], axis=1)
                parts = fold_t(parts, t, tensor_left.pop(0), bf)
                new_up, new_down, parts = lax.optimization_barrier((new_up, new_down, parts))
            if step == FOLD_AT:
                near, far = lax.optimization_barrier((f_near, f_far, up[-1]))[:2]
                folded = fold_core(near, far)
                new_up, new_down, *folded = lax.optimization_barrier((new_up, new_down, *folded))
            if step == FAR_AT:
                ffn_total = fold_far(*lax.optimization_barrier((*folded, up[-1]))[:2])[0]
            if step == FAR_AT + 2:
                new_up, new_down, ffn_total = lax.optimization_barrier((new_up, new_down, ffn_total))
            if step == FIRST_AT:
                new_up, new_down, half_sums[0] = lax.optimization_barrier((new_up, new_down, half_sums[0]))
            if step == SPREAD_AT:
                new_up, new_down, half_sums[1] = lax.optimization_barrier((new_up, new_down, half_sums[1]))
                totals = spread(half_sums)
            up.append(new_up)
            down.append(new_down)
        output = (mixed + ffn_total).astype(bf)
        for bit in left:
            keep = keep + (flip(send, bit) if got is None else got).astype(f32)
            got = None
            cut = keep.shape[1] // 2
            if cut >= part:
                keep, send = keep[:, :cut], keep[:, cut:].astype(bf)
        if parts is None:
            gain_sums = jnp.broadcast_to(keep[3 * wide : 3 * wide + 16], (n_t, 16, part))
            parts = jnp.concatenate([keep[3 * wide + 16 :].reshape(n_t, wide, part), gain_sums], axis=1)
        for bit in tensor_left:
            parts = fold_t(parts, t, bit, bf)
        mine = parts[0]
        grad_normed1 = jnp.concatenate([up[-1], down[-1]])
        input_grad = (grad_mixed + norm_back(grad_normed1, resid, scale1, gain1)).astype(bf)
        grad_query, grad_key, grad_value = (keep[k * wide : (k + 1) * wide].T for k in range(3))
        grad_out = mine[:wide]
        share = part // n_t
        grad_norm1 = take(mine[wide], t * share, share, 0)
        grad_norm2 = take(mine[wide + 1], t * share, share, 0)

        full = blank((3, n_ff, hid, part), f32)
        for k in range(n_ff):
            full = put(full, totals[k], (d ^ k) % n_ff, 1)
        full = full.reshape(3, hid_t, part)

        return (
            output, input_grad, grad_query, grad_key, grad_value, grad_out,
            full[0].T, full[1].T, full[2], grad_norm1, grad_norm2,
        )

    return on_device


def solution(mesh):
    rows = P(("dp", "tensor"), None)
    return jax.shard_map(
        make(mesh.shape["dp"], mesh.shape["tensor"]),
        mesh=mesh,
        in_specs=(
            rows, P("dp"), P("dp"), P("dp"), P("dp", "tensor"), P("dp", "tensor"),
            P("dp", "tensor"), P("tensor", "dp"), P("dp"), P("dp", "tensor"),
            P("dp", "tensor"), P("tensor", "dp"), rows,
        ),
        out_specs=(
            rows, rows, P("dp", "tensor"), P("dp", "tensor"), P("dp", "tensor"),
            P("tensor", "dp"), P("dp", "tensor"), P("dp", "tensor"), P("tensor", "dp"),
            P(("dp", "tensor")), P(("dp", "tensor")),
        ),
        check_vma=False,
    )
```
